32 devices in a mesh: segment: 4 (over x, core), hid: 4 (over z), wid: 2 (over y).
Axes of the slice: x: 2, y: 2, z: 4, core: 2. Of those that a mesh axis runs over, the one named last changes fastest.
Arguments:
- fwd_input: float32 [128, 5376], P('hid', 'wid'), may hold values from -90 to 90
- saved: float32 [4, 128, 5376], P('segment', 'hid', 'wid'), may hold values from -90 to 90
- cotan: float32 [128, 5376], P('hid', 'wid'), may hold values from -12 to 12
- norm_gain: float32 [4, 5376], P('segment', 'wid'), may hold values from 0.1 to 1.9
- w_gate: bfloat16 [4, 5376, 21504], P('segment', 'wid', 'hid'), may hold values from -0.078125 to 0.078125
- w_up: bfloat16 [4, 5376, 21504], P('segment', 'wid', 'hid'), may hold values from -1 to 1
- w_down: bfloat16 [4, 21504, 5376], P('segment', 'hid', 'wid'), may hold values from -1 to 1
- adapt_a: bfloat16 [4, 5376, 16], P('segment', 'wid'), may hold values from -0.078125 to 0.078125
- adapt_b: bfloat16 [4, 16, 21504], P('segment', None, 'hid'), may hold values from -1.5 to 1.5
Outputs:
- fwd_out: float32 [4, 128, 5376], P('segment', 'hid', 'wid')
- grad_in: float32 [4, 128, 5376], P('segment', 'hid', 'wid')
- grad_a: float32 [4, 5376, 16], P('segment', 'wid')
- grad_b: float32 [4, 16, 21504], P('segment', None, 'hid')
The draws below stay inside these ranges and needn't reach their ends.
All inputs are finite; a program needn't handle non-finite values.
Results may differ from the reference program's by a relative error of at most 0.009.
Values may be sent and summed in bfloat16 or wider, within the bound.
No kernel may reach another device: no remote copies, remote signals or barrier semaphores. Data moves between devices by JAX's collectives and lax.ppermute only.
A program may use at most 192 MiB of HBM per device.

```python
import math
import jax
import jax.numpy as jnp
from jax import lax

D = 5376
FF = 21504
RANK = 16
ROWS = 128
SEGMENTS = 4


def row_parts(key, leading):
    first_key, second_key, third_key = jax.random.split(key, 3)
    shape = leading + (ROWS, D)
    base_values = jnp.clip(jax.random.normal(first_key, shape, jnp.float32), -4.0, 4.0)
    row_scales = jnp.exp(jax.random.uniform(second_key, leading + (ROWS, 1), jnp.float32, jnp.log(0.5), jnp.log(5.0)))
    column_ramp = 1.0 + 2.0 * jnp.arange(D, dtype=jnp.float32) / (D - 1)
    column_scales = column_ramp * jnp.exp(jax.random.uniform(third_key, (D,), jnp.float32, -0.35, 0.35))
    return (base_values, row_scales, column_scales)


def scaled_rows(key, leading):
    base_values, row_scales, column_scales = row_parts(key, leading)
    return base_values * row_scales * column_scales


def stream_base(key):
    return row_parts(jax.random.fold_in(key, 12), ())


def draw_fwd_input(key, part):
    return scaled_rows(jax.random.fold_in(key, 11), ())


def draw_saved(key, part):
    base_values, row_scales, column_scales = stream_base(key)
    common = base_values * row_scales * column_scales
    extra = scaled_rows(jax.random.fold_in(key, 14), (SEGMENTS,))
    return 0.7 * common[None] + 0.35 * extra


def draw_cotan(key, part):
    base_values, row_scales, column_scales = stream_base(key)
    noise = jnp.clip(jax.random.normal(jax.random.fold_in(key, 13), (ROWS, D), jnp.float32), -6.0, 6.0)
    return 0.6 * noise + 0.4 * base_values * column_scales


def unit_entries(segment_key, shape):
    return jnp.clip(jax.random.normal(segment_key, shape, jnp.float32), -4.0, 4.0)


def shared_source(key, segment):
    return unit_entries(jax.random.fold_in(jax.random.fold_in(key, 21), segment), (D, FF))


def draw_w_up(key, part):
    segment_ids = jnp.arange(SEGMENTS, dtype=jnp.int32)
    return lax.map(lambda segment: shared_source(key, segment) * (1.0 / math.sqrt(D)), segment_ids).astype(jnp.bfloat16)


def draw_w_down(key, part):
    segment_ids = jnp.arange(SEGMENTS, dtype=jnp.int32)

    def one_segment(segment):
        own = unit_entries(jax.random.fold_in(jax.random.fold_in(key, 22), segment), (FF, D))
        return (0.8 * shared_source(key, segment).T + 0.6 * own) * (1.0 / math.sqrt(FF))
    return lax.map(one_segment, segment_ids).astype(jnp.bfloat16)


def block_levels(key, shape, shards, least, largest):
    level, own = 1.0, jax.random.fold_in(key, 6)
    for axis_at, blocks in shards:
        draws = jnp.exp(jax.random.uniform(jax.random.fold_in(own, axis_at), (blocks,), jnp.float32, least / len(shards), largest / len(shards)))
        level = level * jnp.repeat(draws, shape[axis_at] // blocks).reshape([-1 if axis == axis_at else 1 for axis in range(len(shape))])
    return level


def bell_draw(stream_key, shape, width, most, cuts=(), held_as=jnp.bfloat16):
    array = jax.random.normal(stream_key, shape, jnp.float32) * width
    if len(cuts) > 0:
        array = block_levels(stream_key, shape, cuts, -0.22, 0.18) * array
    return jnp.clip(array, min=-most, max=most).astype(held_as)


def setup_inputs(seed: int = 0) -> dict:
    splits = jax.random.split(jax.random.key(seed), 10)
    return {
        "fwd_input": draw_fwd_input(jax.random.fold_in(splits[9], 71), 0),
        "saved": draw_saved(jax.random.fold_in(splits[9], 71), 0),
        "cotan": draw_cotan(jax.random.fold_in(splits[9], 71), 0),
        "norm_gain": jnp.clip(1.0 + 0.18 * jax.random.normal(splits[3], (SEGMENTS, D), jnp.float32), 0.1, 1.9),
        "w_gate": bell_draw(splits[4], (SEGMENTS, D, FF), D ** -0.5, 0.078125, ((0, 4), (1, 2), (2, 4))),
        "w_up": draw_w_up(jax.random.fold_in(splits[9], 71), 0),
        "w_down": draw_w_down(jax.random.fold_in(splits[9], 71), 0),
        "adapt_a": bell_draw(splits[7], (SEGMENTS, D, RANK), D ** -0.5, 0.078125, ((0, 4), (1, 2))),
        "adapt_b": bell_draw(splits[8], (SEGMENTS, RANK, FF), RANK ** -0.5, 1.5, ((0, 4), (2, 4))),
    }


epsilon = 1e-06
highest = lax.Precision.HIGHEST
ACROSS = (((1,), (1,)), ((), ()))
DOWN_ROWS = (((0,), (0,)), ((), ()))

def gelu_pair(values):
    active, pullback = jax.vjp(lambda inner: jax.nn.gelu(inner, approximate=True), values)
    return (active, pullback(jnp.ones_like(values))[0])

def normalize(inputs, scales):
    inverse = lax.rsqrt(lax.optimization_barrier(jnp.sum(inputs * inputs, axis=1, keepdims=True)) / D + epsilon)
    return (inverse, (inputs * inverse * scales).astype(jnp.bfloat16))

def project(normed, gate_weights, up_weights, adapter_a, adapter_b):
    gate_pre = jnp.dot(normed, gate_weights, preferred_element_type=jnp.float32)
    up_pre = jnp.dot(normed, up_weights, preferred_element_type=jnp.float32)
    low_rank = jnp.dot(normed, adapter_a, preferred_element_type=jnp.float32)
    low_round = low_rank.astype(jnp.bfloat16)
    upward = up_pre + jnp.dot(low_round, adapter_b, preferred_element_type=jnp.float32)
    return (gate_pre, upward, low_round)

def reference(fwd_input, saved, cotan, norm_gain, w_gate, w_up, w_down, adapt_a, adapt_b):
    outputs = []
    current = fwd_input
    for section in range(SEGMENTS):
        inverse, normed = normalize(current, norm_gain[section])
        gate_pre, upward, low_round = project(normed, w_gate[section], w_up[section], adapt_a[section], adapt_b[section])
        hidden = (jax.nn.gelu(gate_pre, approximate=True) * upward).astype(jnp.bfloat16)
        current = current + jnp.dot(hidden, w_down[section], preferred_element_type=jnp.float32)
        outputs.append(current)
    grads_in = [None] * SEGMENTS
    grads_a = [None] * SEGMENTS
    grads_b = [None] * SEGMENTS
    grad_y = cotan
    for section in reversed(range(SEGMENTS)):
        inputs = saved[section]
        scales = norm_gain[section]
        inverse, normed = normalize(inputs, scales)
        gate_pre, upward, low_round = project(normed, w_gate[section], w_up[section], adapt_a[section], adapt_b[section])
        grad_round = grad_y.astype(jnp.bfloat16)
        grad_hidden = lax.dot_general(grad_round, w_down[section], ACROSS, preferred_element_type=jnp.float32)
        active, slopes = gelu_pair(gate_pre)
        grad_gate = (grad_hidden * upward * slopes).astype(jnp.bfloat16)
        grad_up = (grad_hidden * active).astype(jnp.bfloat16)
        grad_low = lax.dot_general(grad_up, adapt_b[section], ACROSS, preferred_element_type=jnp.float32)
        grad_norm = lax.dot_general(grad_gate, w_gate[section], ACROSS, preferred_element_type=jnp.float32)
        grad_norm = grad_norm + lax.dot_general(grad_up, w_up[section], ACROSS, preferred_element_type=jnp.float32)
        grad_norm = grad_norm + jnp.dot(grad_low, adapt_a[section].astype(jnp.float32).T, precision=highest)
        weighted = lax.optimization_barrier(jnp.sum(grad_norm * scales * inputs, axis=1, keepdims=True))
        grad_y = grad_y + inverse * scales * grad_norm - inputs * (inverse * inverse * inverse) * weighted / D
        grads_in[section] = grad_y
        grads_a[section] = jnp.dot(normed.astype(jnp.float32).T, grad_low, precision=highest)
        grads_b[section] = lax.dot_general(low_round, grad_up, DOWN_ROWS, preferred_element_type=jnp.float32)
    return (jnp.stack(outputs), jnp.stack(grads_in), jnp.stack(grads_a), jnp.stack(grads_b))
```

```python
import functools

import jax
import jax.numpy as jnp
from jax import lax
from jax.experimental import pallas as pl
from jax.experimental.pallas import tpu as pltpu
from jax.sharding import PartitionSpec as P

EPS = 1e-06
DEPTH_FIRST = 2
DEPTH_DOWN = 4
DEPTH_BACK = 2
LANES = 128
AXES = ("segment", "hid", "wid")
NT = (((1,), (1,)), ((), ()))
TN = (((0,), (0,)), ((), ()))
F32 = jnp.float32
BF16 = jnp.bfloat16
ROOT = 0.7978845608028654
CUBIC = 0.044715
VMEM_BYTES = 60000 * 1024
ANY = pl.BlockSpec(memory_space=pl.ANY)
SMEM = pl.BlockSpec(memory_space=pltpu.SMEM)


def block_of(total, most=384):
    best = [d for d in range(LANES, most + 1, LANES) if total % d == 0]
    return best[-1] if best else total


def split3(v):
    hi = v.astype(BF16).astype(F32)
    mid = (v - hi).astype(BF16).astype(F32)
    return hi, mid, (v - hi - mid).astype(BF16).astype(F32)


def at_lanes(shape, first, parts):
    lane = lax.broadcasted_iota(jnp.int32, shape, 1)
    out = jnp.zeros(shape, F32)
    for i, part in enumerate(parts):
        out = jnp.where(lane == first + i, part, out)
    return out


def sum_lanes(v, first, count):
    lane = lax.broadcasted_iota(jnp.int32, v.shape, 1)
    return jnp.sum(jnp.where((lane >= first) & (lane < first + count), v, 0.0), 1, keepdims=True)


def lane_start(i, size):
    return pl.multiple_of(i * size, LANES) if size % LANES == 0 else i * size


def each(blocks, step, carry=0):
    if blocks == 1:
        return step(0, carry)
    return lax.fori_loop(0, blocks, step, carry)


def begin(copies, blocks, depth):
    for i in range(min(depth, blocks)):
        start_all(copies(i))


def arrive(copies, i, blocks, depth):
    wait_all(copies(i))
    if blocks > depth:

        @pl.when(i + depth < blocks)
        def _():
            start_all(copies(i + depth))


def start_all(copies):
    for copy in copies:
        copy.start()


def wait_all(copies):
    for copy in copies:
        copy.wait()


def first_kernel(sz, chunk, skip, mode_ref, *refs):
    refs = refs[skip:]
    n_slots = sz.slot_arrays
    slots = refs[:n_slots]
    wg, wu, wd, a, b, out, grad_out = refs[n_slots:n_slots + 7]
    x_s, a_s, b_s, g_s, u_s, d_s, o_s, e_s, sem_x, sem_g, sem_u, sem_o = refs[n_slots + 7:]
    half, unit, pad = sz.half, sz.chunk_units, sz.unit_pad
    rows = sz.rows // n_slots
    mode = mode_ref[0]
    size = block_of(unit)
    blocks = unit // size
    loads = [
        pltpu.make_async_copy(
            slots[k].at[:, pl.ds(0, half + LANES)],
            x_s.at[pl.ds(k * rows, rows), :],
            sem_x.at[k],
        )
        for k in range(n_slots)
    ]

    def columns(ref, i):
        if blocks == 1:
            return ref.at[0]
        return ref.at[0, :, pl.ds(lane_start(i, size) + chunk * unit, size)]

    @pl.when(mode == 1)
    def _():
        more = [
            pltpu.make_async_copy(a, a_s, sem_x.at[n_slots]),
            pltpu.make_async_copy(b.at[chunk], b_s, sem_x.at[n_slots + 1]),
        ]

        def copies(i):
            return (
                pltpu.make_async_copy(columns(wg, i), g_s.at[i], sem_g.at[i]),
                pltpu.make_async_copy(columns(wu, i), u_s.at[i], sem_u.at[i]),
            )

        def store(i, part):
            where = pl.ds(lane_start(i, size) + part * pad, size if blocks > 1 else pad)
            return pltpu.make_async_copy(o_s.at[:, where], out.at[:, where], sem_o.at[part])

        start_all(loads + more)
        begin(copies, blocks, DEPTH_FIRST)
        wait_all(loads + more)
        low = jnp.dot(x_s[:, :half], a_s[...], preferred_element_type=F32).astype(BF16)
        e_s[...] = low + x_s[:, pl.ds(half, LANES)]
        if chunk == 0:
            tail = pltpu.make_async_copy(e_s, out.at[:, pl.ds(2 * pad, LANES)], sem_o.at[2])
            tail.start()

        def step(i, _):
            arrive(copies, i, blocks, DEPTH_FIRST)
            x = x_s[:, :half]
            gate = jnp.dot(x, g_s[i], preferred_element_type=F32)
            up = jnp.dot(x, u_s[i], preferred_element_type=F32)
            part = b_s[:, pl.ds(lane_start(i, size), size)]
            up = up + jnp.dot(e_s[...][:, : sz.rank], part, preferred_element_type=F32)
            o_s[:, pl.ds(lane_start(i, size), size)] = gate.astype(BF16)
            store(i, 0).start()
            o_s[:, pl.ds(lane_start(i, size) + pad, size)] = up.astype(BF16)
            store(i, 1).start()
            return 0

        each(blocks, step)
        for part in range(2):
            where = pl.ds(part * pad, pad)
            pltpu.make_async_copy(o_s.at[:, where], out.at[:, where], sem_o.at[part]).wait()
        if chunk == 0:
            tail.wait()

    @pl.when(mode == 2)
    def _():
        def copies(i):
            where = pl.ds(i * size + chunk * unit, size)
            return (pltpu.make_async_copy(wd.at[0, where, :], d_s.at[i], sem_g.at[i]),)

        def store(i):
            where = pl.ds(lane_start(i, size), size if blocks > 1 else pad)
            return pltpu.make_async_copy(o_s.at[:, where], grad_out.at[:, where], sem_o.at[0])

        start_all(loads)
        begin(copies, blocks, DEPTH_FIRST)
        wait_all(loads)

        def step(i, _):
            arrive(copies, i, blocks, DEPTH_FIRST)
            o_s[:, pl.ds(lane_start(i, size), size)] = lax.dot_general(
                x_s[:, :half], d_s[i], NT, preferred_element_type=F32
            ).astype(BF16)
            store(i).start()
            return 0

        each(blocks, step)
        where = pl.ds(0, pad)
        pltpu.make_async_copy(o_s.at[:, where], grad_out.at[:, where], sem_o.at[0]).wait()


def first_call(sz, chunk, mode, slots, weights, after=()):
    wg, wu, wd, a, b = weights
    unit, pad = sz.chunk_units, sz.unit_pad
    size = block_of(unit)
    blocks = unit // size
    n = sz.slot_arrays
    return pl.pallas_call(
        functools.partial(first_kernel, sz, chunk, len(after)),
        out_shape=[
            jax.ShapeDtypeStruct((sz.rows, sz.width(chunk)), BF16),
            jax.ShapeDtypeStruct((sz.rows, pad), BF16),
        ],
        in_specs=[SMEM] + [ANY] * (len(after) + n + 5),
        out_specs=[ANY] * 2,
        scratch_shapes=[
            pltpu.VMEM((sz.rows, sz.half + LANES), BF16),
            pltpu.VMEM((sz.half, LANES), BF16),
            pltpu.VMEM((sz.rank, unit), BF16),
            pltpu.VMEM((blocks, sz.half, size), BF16),
            pltpu.VMEM((blocks, sz.half, size), BF16),
            pltpu.VMEM((blocks, size, sz.half), BF16),
            pltpu.VMEM((sz.rows, 2 * pad), BF16),
            pltpu.VMEM((sz.rows, LANES), BF16),
            pltpu.SemaphoreType.DMA((n + 2,)),
            pltpu.SemaphoreType.DMA((blocks,)),
            pltpu.SemaphoreType.DMA((blocks,)),
            pltpu.SemaphoreType.DMA((3,)),
        ],
        compiler_params=pltpu.CompilerParams(vmem_limit_bytes=VMEM_BYTES),
        cost_estimate=pl.CostEstimate(
            flops=4 * sz.rows * sz.half * unit,
            bytes_accessed=4 * sz.half * unit,
            transcendentals=0,
        ),
        name="first%d" % chunk,
    )(mode, *after, *slots, wg, wu, wd, a, b)


def total(ref, where):
    v = ref[0, :, where].astype(F32)
    for j in range(1, ref.shape[0]):
        v = v + ref[j, :, where].astype(F32)
    return v


def inverse_of(sz, extras):
    return lax.rsqrt(sum_lanes(extras, sz.rank, 3) / sz.model + EPS)


def part_copies(sz, main, extra, m_s, e_s, sem):
    out = []
    for j in range(sz.wid):
        out.append(
            pltpu.make_async_copy(
                extra[j].at[:, pl.ds(2 * sz.unit_pad, LANES)], e_s.at[j], sem.at[2 * j]
            )
        )
        out.append(
            pltpu.make_async_copy(
                main[j].at[:, pl.ds(0, 2 * sz.unit_pad)], m_s.at[j], sem.at[2 * j + 1]
            )
        )
    return out


def prepare_kernel(sz, mode_ref, *refs):
    wn = sz.wid
    main, extra = refs[:wn], refs[wn:2 * wn]
    out, stats, m_s, e_s, o_s, t_s, sem, sem_o = refs[2 * wn:]
    unit, pad = sz.chunk_units, sz.unit_pad
    size = block_of(unit)
    blocks = unit // size

    @pl.when(mode_ref[0] == 1)
    def _():
        loads = part_copies(sz, main, extra, m_s, e_s, sem)
        start_all(loads)
        wait_all(loads)
        extras = total(e_s, slice(None))
        inverse = inverse_of(sz, extras)
        lane = lax.broadcasted_iota(jnp.int32, (sz.rows, LANES), 1)
        t_s[...] = jnp.where(lane < sz.rank, extras * inverse, inverse)
        side = pltpu.make_async_copy(t_s, stats, sem_o.at[1])
        side.start()

        def step(i, _):
            where = pl.ds(lane_start(i, size), size)
            gate = total(m_s, where) * inverse
            up = total(m_s, pl.ds(lane_start(i, size) + pad, size)) * inverse
            bend = jnp.tanh(ROOT * (gate + CUBIC * (gate * gate * gate)))
            active = 0.5 * gate * (1.0 + bend)
            slope = 0.5 * (1.0 + bend) + 0.5 * gate * (1.0 - bend * bend) * (
                ROOT * (1.0 + 3.0 * CUBIC * (gate * gate))
            )
            o_s[0, :, where] = up * slope
            o_s[1, :, where] = active
            o_s[2, :, where] = up * (slope * gate + active)
            if blocks > 1:
                pltpu.make_async_copy(
                    o_s.at[:, :, where], out.at[:, :, where], sem_o.at[0]
                ).start()
            return 0

        each(blocks, step)
        done = pltpu.make_async_copy(o_s, out, sem_o.at[0])
        if blocks == 1:
            done.start()
        done.wait()
        side.wait()


def prepare_call(sz, mode, main, extra):
    wn, pad = sz.wid, sz.unit_pad
    return pl.pallas_call(
        functools.partial(prepare_kernel, sz),
        out_shape=[
            jax.ShapeDtypeStruct((3, sz.rows, pad), F32),
            jax.ShapeDtypeStruct((sz.rows, LANES), F32),
        ],
        in_specs=[SMEM] + [ANY] * (2 * wn),
        out_specs=[ANY] * 2,
        scratch_shapes=[
            pltpu.VMEM((wn, sz.rows, 2 * pad), BF16),
            pltpu.VMEM((wn, sz.rows, LANES), BF16),
            pltpu.VMEM((3, sz.rows, pad), F32),
            pltpu.VMEM((sz.rows, LANES), F32),
            pltpu.SemaphoreType.DMA((2 * wn,)),
            pltpu.SemaphoreType.DMA((2,)),
        ],
        compiler_params=pltpu.CompilerParams(vmem_limit_bytes=VMEM_BYTES),
        cost_estimate=pl.CostEstimate(
            flops=40 * sz.rows * pad, bytes_accessed=20 * sz.rows * pad, transcendentals=0
        ),
        name="prepare",
    )(mode, *main, *extra)


def second_kernel(sz, chunk, skip, mode_ref, *refs):
    wn, n, pr = sz.wid, sz.hid, sz.part_rows
    refs = list(refs[skip:])

    def take(count):
        out, refs[:] = refs[:count], refs[count:]
        return out

    first = chunk == 0
    last = chunk == sz.chunks - 1
    p0, pc, d = take(wn), take(wn), take(wn)
    ready, stats, wg, wu, wd, a, b = take(7)
    acc_in = None if first else take(1)[0]
    gb_out = take(1)[0]
    if last:
        own_out = take(1)[0]
        sends = take(sz.send_arrays)
    else:
        acc_out, token = take(2)
    m_s, e_s, d_s, r_s, t_s, h_s, k_s, w_s, g_s, u_s, a_s, b_s, gb_s, acc_s, s_s = take(15)
    sem_i, sem_w, sem_u, sem_o = take(4)
    half, unit, pad = sz.half, sz.chunk_units, sz.unit_pad
    mode = mode_ref[0]
    size, size_h = block_of(unit), block_of(half)
    blocks, blocks_h = unit // size, half // size_h
    carried = [] if first else [pltpu.make_async_copy(acc_in, acc_s, sem_i.at[2 * wn])]

    def write_out():
        if last:
            s_s[...] = acc_s[...].astype(BF16)
            outs = [pltpu.make_async_copy(acc_s.at[pl.ds(0, pr), :], own_out, sem_o.at[0])]
            if sz.slot_arrays == 1:
                outs.append(pltpu.make_async_copy(s_s, sends[0], sem_o.at[1]))
            else:
                for k in range(1, n):
                    outs.append(
                        pltpu.make_async_copy(
                            s_s.at[pl.ds(k * pr, pr), :], sends[k - 1], sem_o.at[k]
                        )
                    )
        else:
            outs = [
                pltpu.make_async_copy(acc_s, acc_out, sem_o.at[0]),
                pltpu.make_async_copy(acc_s.at[pl.ds(0, 8), pl.ds(0, LANES)], token, sem_o.at[1]),
            ]
        start_all(outs)
        wait_all(outs)

    @pl.when(mode == 1)
    def _():
        loads = part_copies(sz, pc, p0, m_s, e_s, sem_i)

        def copies(j):
            return (
                pltpu.make_async_copy(
                    wd.at[0, pl.ds(chunk * unit, unit), pl.ds(lane_start(j, size_h), size_h)],
                    w_s.at[j],
                    sem_w.at[j],
                ),
            )

        start_all(loads)
        start_all(carried)
        begin(copies, blocks_h, DEPTH_DOWN)
        wait_all(loads)
        inverse = inverse_of(sz, total(e_s, slice(None)))

        def act(i, _):
            gate = total(m_s, pl.ds(lane_start(i, size), size)) * inverse
            up = total(m_s, pl.ds(lane_start(i, size) + pad, size)) * inverse
            bend = jnp.tanh(ROOT * (gate + CUBIC * (gate * gate * gate)))
            h_s[:, pl.ds(lane_start(i, size), size)] = (
                0.5 * gate * (1.0 + bend) * up
            ).astype(BF16)
            return 0

        each(blocks, act)
        wait_all(carried)

        def step(j, _):
            arrive(copies, j, blocks_h, DEPTH_DOWN)
            where = pl.ds(lane_start(j, size_h), size_h)
            v = jnp.dot(h_s[...], w_s[j], preferred_element_type=F32)
            acc_s[:, where] = v if first else acc_s[:, where] + v
            return 0

        each(blocks_h, step)
        write_out()

    @pl.when(mode == 2)
    def _():
        loads = [pltpu.make_async_copy(ready, r_s, sem_i.at[2 * wn + 1])] + [
            pltpu.make_async_copy(d[j], d_s.at[j], sem_i.at[j]) for j in range(wn)
        ]
        more = [
            pltpu.make_async_copy(stats, t_s, sem_i.at[2 * wn + 2]),
            pltpu.make_async_copy(a, a_s, sem_i.at[2 * wn + 3]),
            pltpu.make_async_copy(b.at[chunk], b_s, sem_i.at[2 * wn + 4]),
        ]

        def copies(j):
            rows = pl.ds(j * size_h, size_h)
            cols = pl.ds(chunk * unit, unit)
            return (
                pltpu.make_async_copy(wg.at[0, rows, cols], g_s.at[j], sem_w.at[j]),
                pltpu.make_async_copy(wu.at[0, rows, cols], u_s.at[j], sem_u.at[j]),
            )

        start_all(loads)
        start_all(more)
        start_all(carried)
        begin(copies, blocks_h, DEPTH_BACK)
        wait_all(loads)

        def act(i, inner):
            where = pl.ds(lane_start(i, size), size)
            grad = total(d_s, where)
            h_s[:, where] = (grad * r_s[0, :, where]).astype(BF16)
            k_s[:, where] = (grad * r_s[1, :, where]).astype(BF16)
            return inner + jnp.sum(grad * r_s[2, :, where], 1, keepdims=True)

        inner = each(blocks, act, jnp.zeros((sz.rows, 1), F32))
        wait_all(more)
        wait_all(carried)
        low = t_s[...].astype(BF16)[:, : sz.rank]
        inverse = t_s[...][:, sz.rank:sz.rank + 1]
        grad_low = lax.dot_general(k_s[...], b_s[...], NT, preferred_element_type=F32)
        low_hi, low_mid, _ = split3(grad_low)
        low_hi, low_mid = low_hi.astype(BF16), low_mid.astype(BF16)

        def step(j, _):
            arrive(copies, j, blocks_h, DEPTH_BACK)
            where = pl.ds(lane_start(j, size_h), size_h)
            v = lax.dot_general(h_s[...], g_s[j], NT, preferred_element_type=F32)
            v = v + lax.dot_general(k_s[...], u_s[j], NT, preferred_element_type=F32)
            a_block = a_s[pl.ds(j * size_h, size_h), :][:, : sz.rank]
            v = v + lax.dot_general(low_hi, a_block, NT, preferred_element_type=F32)
            v = v + lax.dot_general(low_mid, a_block, NT, preferred_element_type=F32)
            acc_s[:, where] = v if first else acc_s[:, where] + v
            return 0

        each(blocks_h, step)
        gb_s[...] = lax.dot_general(low, k_s[...], TN, preferred_element_type=F32)
        out_b = pltpu.make_async_copy(gb_s, gb_out, sem_i.at[2 * wn + 5])
        out_b.start()
        if not first:
            inner = inner + acc_s[:, pl.ds(half, LANES)][:, :1]
            grad_low = grad_low + acc_s[:, pl.ds(half + LANES, LANES)][:, : sz.rank]
        if last:
            acc_s[:, pl.ds(half, LANES)] = at_lanes(
                (sz.rows, LANES), 0, split3(inner) + (inverse,)
            )
            hi, mid, _ = split3(grad_low * inverse)
            spread = jnp.zeros((pr, sz.low_lanes), F32)
            r_i = lax.broadcasted_iota(jnp.int32, (sz.rank, sz.low_lanes), 0)
            l_i = lax.broadcasted_iota(jnp.int32, (sz.rank, sz.low_lanes), 1)
            for j in range(n):
                for part, first_lane in ((hi, 2 * j * sz.rank), (mid, (2 * j + 1) * sz.rank)):
                    pick = jnp.where(l_i == r_i + first_lane, 1.0, 0.0).astype(BF16)
                    spread = spread + jnp.dot(
                        part[j * pr:(j + 1) * pr].astype(BF16), pick, preferred_element_type=F32
                    )
            for j in range(n):
                acc_s[pl.ds(j * pr, pr), pl.ds(half + LANES, sz.low_lanes)] = spread
        else:
            acc_s[:, pl.ds(half, LANES)] = at_lanes((sz.rows, LANES), 0, (inner,))
            r_i = lax.broadcasted_iota(jnp.int32, (sz.rank, LANES), 0)
            l_i = lax.broadcasted_iota(jnp.int32, (sz.rank, LANES), 1)
            pick = jnp.where(l_i == r_i, 1.0, 0.0).astype(BF16)
            wide = jnp.zeros((sz.rows, LANES), F32)
            for part in split3(grad_low):
                wide = wide + jnp.dot(part.astype(BF16), pick, preferred_element_type=F32)
            acc_s[:, pl.ds(half + LANES, LANES)] = wide
        write_out()
        out_b.wait()


def second_call(sz, chunk, mode, p0, pc, d, ready, stats, weights, acc, after=()):
    wg, wu, wd, a, b = weights
    wn, n, pr = sz.wid, sz.hid, sz.part_rows
    unit, half, pad = sz.chunk_units, sz.half, sz.unit_pad
    last = chunk == sz.chunks - 1
    size_h = block_of(half)
    blocks_h = half // size_h
    wide = half + LANES + sz.low_lanes
    shapes = [jax.ShapeDtypeStruct((sz.rank, unit), F32)]
    if last:
        shapes.append(jax.ShapeDtypeStruct((pr, wide), F32))
        if sz.slot_arrays == n:
            shapes += [jax.ShapeDtypeStruct((pr, wide), BF16)] * (n - 1)
        else:
            shapes.append(jax.ShapeDtypeStruct((sz.rows, wide), BF16))
    else:
        shapes.append(jax.ShapeDtypeStruct((sz.rows, wide), F32))
        shapes.append(jax.ShapeDtypeStruct((8, LANES), F32))
    operands = [mode, *after, *p0, *pc, *d, ready, stats, wg, wu, wd, a, b]
    if chunk > 0:
        operands.append(acc)
    return pl.pallas_call(
        functools.partial(second_kernel, sz, chunk, len(after)),
        out_shape=shapes,
        in_specs=[SMEM] + [ANY] * (len(operands) - 1),
        out_specs=[ANY] * len(shapes),
        scratch_shapes=[
            pltpu.VMEM((wn, sz.rows, 2 * pad), BF16),
            pltpu.VMEM((wn, sz.rows, LANES), BF16),
            pltpu.VMEM((wn, sz.rows, pad), BF16),
            pltpu.VMEM((3, sz.rows, pad), F32),
            pltpu.VMEM((sz.rows, LANES), F32),
            pltpu.VMEM((sz.rows, unit), BF16),
            pltpu.VMEM((sz.rows, unit), BF16),
            pltpu.VMEM((blocks_h, unit, size_h), BF16),
            pltpu.VMEM((blocks_h, size_h, unit), BF16),
            pltpu.VMEM((blocks_h, size_h, unit), BF16),
            pltpu.VMEM((half, LANES), BF16),
            pltpu.VMEM((sz.rank, unit), BF16),
            pltpu.VMEM((sz.rank, unit), F32),
            pltpu.VMEM((sz.rows, wide), F32),
            pltpu.VMEM((sz.rows, wide), BF16),
            pltpu.SemaphoreType.DMA((2 * wn + 6,)),
            pltpu.SemaphoreType.DMA((blocks_h,)),
            pltpu.SemaphoreType.DMA((blocks_h,)),
            pltpu.SemaphoreType.DMA((max(n, 2),)),
        ],
        compiler_params=pltpu.CompilerParams(vmem_limit_bytes=VMEM_BYTES),
        cost_estimate=pl.CostEstimate(
            flops=4 * sz.rows * half * unit, bytes_accessed=4 * half * unit, transcendentals=0
        ),
        name="second%d" % chunk,
    )(*operands)


def finish_kernel(sz, skip, mode_ref, *refs):
    refs = refs[skip:]
    n, half = sz.hid, sz.half
    own = refs[0]
    got = refs[1:n]
    prev, saved, gain, gain_next, out, payload, carry, low_out = refs[n:]
    mode = mode_ref[0]

    def before():
        if prev.shape[1] == half:
            return prev[...]
        return (
            prev[:, pl.ds(half + LANES, half)].astype(F32)
            + prev[:, pl.ds(2 * half + LANES, half)].astype(F32)
        )

    def send(scaled, tail, v):
        payload[:, :half] = scaled
        payload[:, pl.ds(half, LANES)] = tail
        carry[:, :half] = scaled
        carry[:, pl.ds(half, LANES)] = tail
        hi = v.astype(BF16)
        carry[:, pl.ds(half + LANES, half)] = hi
        carry[:, pl.ds(2 * half + LANES, half)] = (v - hi.astype(F32)).astype(BF16)

    def summed():
        v = own[:, :half]
        for ref in got:
            v = v + ref[:, :half].astype(F32)
        return v

    @pl.when(mode == 1)
    def _():
        v = before() + summed()
        out[...] = v
        squares = jnp.sum(v * v, 1, keepdims=True)
        tail = at_lanes((sz.part_rows, LANES), sz.rank, split3(squares)).astype(BF16)
        send((v * gain_next[...]).astype(BF16), tail, v)

    @pl.when(mode == 2)
    def _():
        marks = own[:, pl.ds(half, LANES)]
        inverse = sum_lanes(marks, 3, 1)
        low = own[:, pl.ds(half + LANES, sz.low_lanes)]
        for k, ref in enumerate(got):
            marks = marks + ref[:, pl.ds(half, LANES)].astype(F32)
            part = ref[:, pl.ds(half + LANES, sz.low_lanes)].astype(F32)
            low = low + pltpu.roll(part, sz.low_lanes - (k + 1) * 2 * sz.rank, 1)
        inner = sum_lanes(marks, 0, 3)
        factor = inverse * inverse * inner / sz.model
        v = before() + inverse * gain[...] * summed() - saved[...] * factor
        out[...] = v
        send(v.astype(BF16), jnp.zeros((sz.part_rows, LANES), BF16), v)
        low_out[...] = low


def finish_call(sz, mode, own, got, prev, saved, gain, gain_next, after=()):
    vm = pl.BlockSpec(memory_space=pltpu.VMEM)
    pr, half = sz.part_rows, sz.half
    return pl.pallas_call(
        functools.partial(finish_kernel, sz, len(after)),
        out_shape=[
            jax.ShapeDtypeStruct((pr, half), F32),
            jax.ShapeDtypeStruct((pr, half + LANES), BF16),
            jax.ShapeDtypeStruct((pr, 3 * half + LANES), BF16),
            jax.ShapeDtypeStruct((pr, sz.low_lanes), F32),
        ],
        in_specs=[SMEM] + [ANY] * len(after) + [vm] * (sz.hid + 4),
        out_specs=[vm] * 4,
        name="finish",
    )(mode, *after, own, *got, prev, saved, gain, gain_next)


class Sizes:
    def __init__(self, mesh_sizes, part_rows, half, units, rank):
        self.seg, self.hid, self.wid = mesh_sizes
        self.part_rows, self.half, self.units, self.rank = part_rows, half, units, rank
        self.rows = part_rows * self.hid
        self.model = half * self.wid
        self.chunks = 2 if units % (2 * LANES) == 0 else 1
        self.chunk_units = units // self.chunks
        aligned = part_rows % 16 == 0
        self.unit_pad = -(-self.chunk_units // LANES) * LANES
        self.slot_arrays = self.hid if aligned else 1
        self.send_arrays = self.hid - 1 if aligned else 1
        self.low_lanes = 2 * rank * self.hid
        if self.low_lanes % LANES or self.seg < 4 or self.seg % 2:
            raise ValueError("unsupported mesh")

    def width(self, chunk):
        return 2 * self.unit_pad + (LANES if chunk == 0 else 0)

    def index(self, s, h, w):
        return (s * self.hid + h) * self.wid + w


def body(fwd_input, saved, cotan, norm_gain, w_gate, w_up, w_down, adapt_a, adapt_b):
    sizes = tuple(lax.axis_size(axis) for axis in AXES)
    section = lax.axis_index("segment")
    saved_rows = saved[0]
    part_rows, half = fwd_input.shape
    rank, units = adapt_b.shape[1:]
    sz = Sizes(sizes, part_rows, half, units, rank)
    seg, n, wn = sizes
    last = seg - 1
    weights = (
        w_gate, w_up, w_down, jnp.pad(adapt_a[0], ((0, 0), (0, LANES - rank))),
        jnp.stack(jnp.split(adapt_b[0], sz.chunks, 1)),
    )

    def route(block, moves, hid_shift=0, wid_shift=0):
        pairs = [
            (sz.index(s, h, w), sz.index(t, (h + hid_shift) % n, (w + wid_shift) % wn))
            for s, t in moves for h in range(n) for w in range(wn)
        ]
        return lax.ppermute(block, AXES, pairs)

    def stay(sections):
        return [(s, s) for s in sections]

    def rows_of(block, sections):
        return [block] + [route(block, stay(sections), k) for k in range(1, n)]

    def operands(slots):
        if sz.slot_arrays == n:
            return slots
        return [jnp.concatenate(slots)]

    def exchange(block, sections):
        return [block] + [route(block, stay(sections), 0, k) for k in range(1, wn)]

    def flag(*cases):
        mode = jnp.zeros((1,), jnp.int32)
        for value, sections in cases:
            for s in sections:
                mode = jnp.where(section == s, value, mode)
        return mode

    def pack(x, scale):
        squares = jnp.sum(x * x, 1, keepdims=True)
        hi = lax.reduce_precision(squares, 8, 7)
        mid = lax.reduce_precision(squares - hi, 8, 7)
        low = lax.reduce_precision(squares - hi - mid, 8, 7)
        tail = jnp.concatenate([hi, mid, low], 1)
        tail = jnp.pad(tail, ((0, 0), (rank, LANES - rank - 3)))
        return jnp.concatenate([x * scale, tail], 1).astype(BF16)

    def again_of(sections, parts):
        mode = flag((1, sections))
        made = [prepare_call(sz, mode, part, parts[0]) for part in parts]
        return [m[0] for m in made], made[0][1]

    def firsts(modes, slots, after=()):
        made = []
        for c, mode in enumerate(modes):
            made.append(first_call(sz, c, mode, slots, weights, after))
            after = made[-1][:1]
        return [m[0] for m in made], [m[1] for m in made]

    both = range(sz.chunks)
    gain = norm_gain
    begin_rows = jnp.where(section == 0, fwd_input, saved_rows)
    own_rows = rows_of(pack(begin_rows, gain), (0, last))
    slots = operands(own_rows)
    cot = jnp.pad(cotan, ((0, 0), (0, LANES))).astype(BF16)
    cot_slots = operands(rows_of(cot, (last,)))

    made, grad_made, after = [], [], ()
    for c in both:
        made.append(first_call(sz, c, flag((1, (0, last))), slots, weights, after)[0])
        grad_made.append(
            first_call(sz, c, flag((2, (last,))), cot_slots, weights, made[-1:])[1]
        )
        after = grad_made[-1:]
    fwd_parts = [exchange(m, (0, last)) for m in made]
    grad_parts = [exchange(m, (last,)) for m in grad_made]
    again, stats = again_of((last,), fwd_parts)
    gain_next = gain
    for s in range(last):
        back = last - 1 - s
        moved = route(gain, [(back, back + 1), (s + 1, s)])
        gain_next = jnp.where(section == s, moved, gain_next)

    packed = pack(saved_rows, gain)
    middle = tuple(range(1, last))
    mid_rows = rows_of(packed, middle)

    prev = jnp.where(section == 0, fwd_input, cotan)
    outs, lows, grad_bs = [], [], []
    after = ()
    for moment in range(seg):
        ahead, behind = moment, last - moment
        active = (ahead, behind)
        mode = flag((1, (ahead,)), (2, (behind,)))
        if moment > 0:
            made, grad_made = firsts([mode] * sz.chunks, slots, after)
            fwd_parts = [exchange(m, (ahead,)) for m in made]
            grad_parts = [exchange(m, (behind,)) for m in grad_made]
        acc, pieces_b, start, follow = None, [], None, ()
        for c in both:
            res = second_call(
                sz, c, mode, fwd_parts[0], fwd_parts[c], grad_parts[c], again[c], stats,
                weights, acc, follow,
            )
            pieces_b.append(res[0])
            if c < sz.chunks - 1:
                acc = res[1]
                if moment < 2:
                    moves = [(0, 1), (last, last - 1)] if moment == 0 else [(last - 1, last), (1, 0)]
                    start = route(res[2], moves)
                    follow = (start,)
        own, sends = res[1], res[2:]
        if sz.slot_arrays != n:
            sends = [sends[0][k * part_rows:(k + 1) * part_rows] for k in range(1, n)]
        got = [route(sends[k - 1], stay(active), -k) for k in range(1, n)]

        wait = ()
        if moment < 2:
            idle = middle if moment == 0 else (0,)
            source = mid_rows if moment == 0 else first_rows
            redo, _ = firsts(
                [flag((1, idle))] * sz.chunks, operands(source), follow + (own,)
            )
            parts = [exchange(m, idle) for m in redo]
            wait = tuple(redo)
        out, payload, carry, low = finish_call(
            sz, mode, own, got, prev, saved_rows, gain, gain_next, wait
        )
        outs.append(out)
        lows.append(low)
        grad_bs.append(jnp.concatenate(pieces_b, 1))
        if moment < last:
            moves = [(ahead, ahead + 1), (behind, behind - 1)]
            prev = route(carry, moves)
            got = [prev] + [route(payload, moves, k) for k in range(1, n)]
            if sz.slot_arrays != n:
                got = [x[:, : half + LANES] for x in got]
            slots = operands(got)
            after = ()
        if moment == 0:
            again, stats = again_of(idle, parts)
            after += tuple(again)
            held, _ = lax.optimization_barrier((packed, out))
            first_rows = rows_of(held, (0, last))
        elif moment == 1:
            kept = again_of(idle, parts)
            after += tuple(kept[0])
        if moment == last - 1:
            again, stats = kept

    def choose(values, of):
        result = values[0]
        for moment in range(1, seg):
            result = jnp.where(section == of(moment), values[moment], result)
        return result

    fwd_out = choose(outs, lambda m: m)
    grad_in = choose(outs, lambda m: last - m)
    grad_b = choose(grad_bs, lambda m: last - m)
    low = choose(lows, lambda m: last - m)
    low = low.reshape(part_rows, n, 2, rank).sum(2)
    low = jnp.concatenate([low[:, k] for k in range(n)], 0)
    normed = jnp.concatenate(
        [
            jnp.where(
                section == last, x[:, :half], jnp.where(section == 0, z[:, :half], y[:, :half])
            )
            for x, y, z in zip(own_rows, mid_rows, first_rows)
        ],
        0,
    )
    grad_a = lax.dot_general(
        normed.astype(F32), low, TN, precision=lax.Precision.HIGHEST,
        preferred_element_type=F32,
    )
    return (fwd_out[None], grad_in[None], grad_a[None], grad_b[None])


def solution(mesh):
    placed = (
        P("hid", "wid"),
        P("segment", "hid", "wid"),
        P("hid", "wid"),
        P("segment", "wid"),
        P("segment", "wid", "hid"),
        P("segment", "wid", "hid"),
        P("segment", "hid", "wid"),
        P("segment", "wid", None),
        P("segment", None, "hid"),
    )
    return jax.shard_map(
        body,
        mesh=mesh,
        in_specs=placed,
        out_specs=(
            P("segment", "hid", "wid"),
            P("segment", "hid", "wid"),
            P("segment", "wid", None),
            P("segment", None, "hid"),
        ),
        check_vma=False,
    )
```

```python
import functools

import jax
import jax.numpy as jnp
from jax import lax
from jax.experimental import pallas as pl
from jax.experimental.pallas import tpu as pltpu
from jax.sharding import PartitionSpec as P


EPS = 1e-06
FIRST_COST = 16
DEPTH_FIRST = 2
MIB = 1 << 20
DEPTH_DOWN = 4
DEPTH_BACK = 2
LANES = 128
AXES = ("segment", "hid", "wid")
NT = (((1,), (1,)), ((), ()))
TN = (((0,), (0,)), ((), ()))
F32 = jnp.float32
BF16 = jnp.bfloat16
ROOT = 0.7978845608028654
CUBIC = 0.044715
ANY = pl.BlockSpec(memory_space=pl.ANY)
SMEM = pl.BlockSpec(memory_space=pltpu.SMEM)


def block_of(total, most=384):
    best = [d for d in range(LANES, most + 1, LANES) if total % d == 0]
    return best[-1] if best else total


def split3(v):
    hi = v.astype(BF16).astype(F32)
    mid = (v - hi).astype(BF16).astype(F32)
    return hi, mid, (v - hi - mid).astype(BF16).astype(F32)


def at_lanes(shape, first, parts):
    lane = lax.broadcasted_iota(jnp.int32, shape, 1)
    out = jnp.zeros(shape, F32)
    for i, part in enumerate(parts):
        out = jnp.where(lane == first + i, part, out)
    return out


def sum_lanes(v, first, count):
    lane = lax.broadcasted_iota(jnp.int32, v.shape, 1)
    return jnp.sum(jnp.where((lane >= first) & (lane < first + count), v, 0.0), 1, keepdims=True)


def lane_start(i, size):
    return pl.multiple_of(i * size, LANES) if size % LANES == 0 else i * size


def each(blocks, step, carry=0):
    if blocks == 1:
        return step(0, carry)
    return lax.fori_loop(0, blocks, step, carry)


def slots_of(depth, blocks):
    return min(depth + 1, blocks)


def begin(copies, blocks, depth):
    for i in range(min(depth, blocks)):
        start_all(copies(i))


def arrive(copies, i, blocks, depth):
    wait_all(copies(i))
    if blocks > depth:

        @pl.when(i + depth < blocks)
        def _():
            start_all(copies(i + depth))


def start_all(copies):
    for copy in copies:
        copy.start()


def wait_all(copies):
    for copy in copies:
        copy.wait()


def first_kernel(sz, chunk, skip, scaled, mode_ref, *refs):
    refs = refs[skip:]
    n_slots = sz.slot_arrays
    slots = refs[:n_slots]
    wg, wu, wd, a, b = refs[n_slots:n_slots + 5]
    refs = refs[n_slots + 5:]
    gain = refs[0] if scaled else None
    out, grad_out, x_s, a_s, b_s, g_s, u_s, d_s, o_s, e_s, n_s, sem_x, sem_g, sem_u, sem_o = (
        refs[1:] if scaled else refs
    )
    half, unit, pad = sz.half, sz.chunk_units, sz.unit_pad
    rows = sz.rows // n_slots
    mode = mode_ref[0]
    size = block_of(unit)
    blocks = unit // size
    ring = slots_of(DEPTH_FIRST, blocks)
    loads = [
        pltpu.make_async_copy(
            slots[k].at[:, pl.ds(0, half + LANES)],
            x_s.at[pl.ds(k * rows, rows), :],
            sem_x.at[k],
        )
        for k in range(n_slots)
    ]

    def columns(ref, i):
        if blocks == 1:
            return ref.at[0]
        return ref.at[0, :, pl.ds(lane_start(i, size) + chunk * unit, size)]

    @pl.when(mode == 1)
    def _():
        more = [
            pltpu.make_async_copy(a, a_s, sem_x.at[n_slots]),
            pltpu.make_async_copy(b.at[chunk], b_s, sem_x.at[n_slots + 1]),
        ]

        def copies(i):
            slot = lax.rem(i, ring)
            return (
                pltpu.make_async_copy(columns(wg, i), g_s.at[slot], sem_g.at[slot]),
                pltpu.make_async_copy(columns(wu, i), u_s.at[slot], sem_u.at[slot]),
            )

        def store(i, part):
            where = pl.ds(lane_start(i, size) + part * pad, size if blocks > 1 else pad)
            return pltpu.make_async_copy(o_s.at[:, where], out.at[:, where], sem_o.at[part])

        if scaled:
            more.append(pltpu.make_async_copy(gain, n_s, sem_x.at[n_slots + 2]))
        start_all(loads + more)
        begin(copies, blocks, DEPTH_FIRST)
        wait_all(loads + more)
        if scaled:
            x_s[:, pl.ds(0, half)] = (x_s[:, :half].astype(F32) * n_s[...]).astype(BF16)
        low = jnp.dot(x_s[:, :half], a_s[...], preferred_element_type=F32).astype(BF16)
        e_s[...] = low + x_s[:, pl.ds(half, LANES)]
        if chunk == 0:
            tail = pltpu.make_async_copy(e_s, out.at[:, pl.ds(2 * pad, LANES)], sem_o.at[2])
            tail.start()

        def step(i, _):
            arrive(copies, i, blocks, DEPTH_FIRST)
            x = x_s[:, :half]
            slot = lax.rem(i, ring)
            gate = jnp.dot(x, g_s[slot], preferred_element_type=F32)
            up = jnp.dot(x, u_s[slot], preferred_element_type=F32)
            part = b_s[:, pl.ds(lane_start(i, size), size)]
            up = up + jnp.dot(e_s[...][:, : sz.rank], part, preferred_element_type=F32)
            o_s[:, pl.ds(lane_start(i, size), size)] = gate.astype(BF16)
            store(i, 0).start()
            o_s[:, pl.ds(lane_start(i, size) + pad, size)] = up.astype(BF16)
            store(i, 1).start()
            return 0

        each(blocks, step)
        for part in range(2):
            where = pl.ds(part * pad, pad)
            pltpu.make_async_copy(o_s.at[:, where], out.at[:, where], sem_o.at[part]).wait()
        if chunk == 0:
            tail.wait()

    @pl.when(mode == 2)
    def _():
        def copies(i):
            where = pl.ds(i * size + chunk * unit, size)
            slot = lax.rem(i, ring)
            return (pltpu.make_async_copy(wd.at[0, where, :], d_s.at[slot], sem_g.at[slot]),)

        def store(i):
            where = pl.ds(lane_start(i, size), size if blocks > 1 else pad)
            return pltpu.make_async_copy(o_s.at[:, where], grad_out.at[:, where], sem_o.at[0])

        start_all(loads)
        begin(copies, blocks, DEPTH_FIRST)
        wait_all(loads)

        def step(i, _):
            arrive(copies, i, blocks, DEPTH_FIRST)
            o_s[:, pl.ds(lane_start(i, size), size)] = lax.dot_general(
                x_s[:, :half], d_s[lax.rem(i, ring)], NT, preferred_element_type=F32
            ).astype(BF16)
            store(i).start()
            return 0

        each(blocks, step)
        where = pl.ds(0, pad)
        pltpu.make_async_copy(o_s.at[:, where], grad_out.at[:, where], sem_o.at[0]).wait()


def first_call(sz, chunk, mode, slots, weights, after=(), gain=None):
    wg, wu, wd, a, b = weights
    unit, pad = sz.chunk_units, sz.unit_pad
    size = block_of(unit)
    blocks = unit // size
    ring = slots_of(DEPTH_FIRST, blocks)
    n = sz.slot_arrays
    extra = () if gain is None else (gain,)
    return pl.pallas_call(
        functools.partial(first_kernel, sz, chunk, len(after), gain is not None),
        out_shape=[
            jax.ShapeDtypeStruct((sz.rows, sz.width(chunk)), BF16),
            jax.ShapeDtypeStruct((sz.rows, pad), BF16),
        ],
        in_specs=[SMEM] + [ANY] * (len(after) + n + 5 + len(extra)),
        out_specs=[ANY] * 2,
        scratch_shapes=[
            pltpu.VMEM((sz.rows, sz.half + LANES), BF16),
            pltpu.VMEM((sz.half, LANES), BF16),
            pltpu.VMEM((sz.rank, unit), BF16),
            pltpu.VMEM((ring, sz.half, size), BF16),
            pltpu.VMEM((ring, sz.half, size), BF16),
            pltpu.VMEM((ring, size, sz.half), BF16),
            pltpu.VMEM((sz.rows, 2 * pad), BF16),
            pltpu.VMEM((sz.rows, LANES), BF16),
            pltpu.VMEM((1, sz.half), F32),
            pltpu.SemaphoreType.DMA((n + 3,)),
            pltpu.SemaphoreType.DMA((ring,)),
            pltpu.SemaphoreType.DMA((ring,)),
            pltpu.SemaphoreType.DMA((3,)),
        ],
        compiler_params=pltpu.CompilerParams(vmem_limit_bytes=26 * MIB),
        cost_estimate=pl.CostEstimate(
            flops=4 * sz.rows * sz.half * unit // FIRST_COST,
            bytes_accessed=4 * sz.half * unit // FIRST_COST,
            transcendentals=0,
        ),
    )(mode, *after, *slots, wg, wu, wd, a, b, *extra)


def total(ref, where):
    v = ref[0, :, where].astype(F32)
    for j in range(1, ref.shape[0]):
        v = v + ref[j, :, where].astype(F32)
    return v


def inverse_of(sz, extras):
    return lax.rsqrt(sum_lanes(extras, sz.rank, 3) / sz.model + EPS)


def part_copies(sz, main, extra, m_s, e_s, sem):
    out = []
    for j in range(sz.wid):
        out.append(
            pltpu.make_async_copy(
                extra[j].at[:, pl.ds(2 * sz.unit_pad, LANES)], e_s.at[j], sem.at[2 * j]
            )
        )
        out.append(
            pltpu.make_async_copy(
                main[j].at[:, pl.ds(0, 2 * sz.unit_pad)], m_s.at[j], sem.at[2 * j + 1]
            )
        )
    return out


def prepare_kernel(sz, mode_ref, *refs):
    wn = sz.wid
    main, extra = refs[:wn], refs[wn:2 * wn]
    out, stats, m_s, e_s, o_s, t_s, sem, sem_o = refs[2 * wn:]
    unit, pad = sz.chunk_units, sz.unit_pad
    size = block_of(unit)
    blocks = unit // size

    @pl.when(mode_ref[0] == 1)
    def _():
        loads = part_copies(sz, main, extra, m_s, e_s, sem)
        start_all(loads)
        wait_all(loads)
        extras = total(e_s, slice(None))
        inverse = inverse_of(sz, extras)
        lane = lax.broadcasted_iota(jnp.int32, (sz.rows, LANES), 1)
        t_s[...] = jnp.where(lane < sz.rank, extras * inverse, inverse)
        side = pltpu.make_async_copy(t_s, stats, sem_o.at[1])
        side.start()

        def step(i, _):
            where = pl.ds(lane_start(i, size), size)
            gate = total(m_s, where) * inverse
            up = total(m_s, pl.ds(lane_start(i, size) + pad, size)) * inverse
            bend = jnp.tanh(ROOT * (gate + CUBIC * (gate * gate * gate)))
            active = 0.5 * gate * (1.0 + bend)
            slope = 0.5 * (1.0 + bend) + 0.5 * gate * (1.0 - bend * bend) * (
                ROOT * (1.0 + 3.0 * CUBIC * (gate * gate))
            )
            o_s[0, :, where] = up * slope
            o_s[1, :, where] = active
            o_s[2, :, where] = up * (slope * gate + active)
            if blocks > 1:
                pltpu.make_async_copy(
                    o_s.at[:, :, where], out.at[:, :, where], sem_o.at[0]
                ).start()
            return 0

        each(blocks, step)
        done = pltpu.make_async_copy(o_s, out, sem_o.at[0])
        if blocks == 1:
            done.start()
        done.wait()
        side.wait()


def prepare_call(sz, mode, main, extra):
    wn, pad = sz.wid, sz.unit_pad
    return pl.pallas_call(
        functools.partial(prepare_kernel, sz),
        out_shape=[
            jax.ShapeDtypeStruct((3, sz.rows, pad), F32),
            jax.ShapeDtypeStruct((sz.rows, LANES), F32),
        ],
        in_specs=[SMEM] + [ANY] * (2 * wn),
        out_specs=[ANY] * 2,
        scratch_shapes=[
            pltpu.VMEM((wn, sz.rows, 2 * pad), BF16),
            pltpu.VMEM((wn, sz.rows, LANES), BF16),
            pltpu.VMEM((3, sz.rows, pad), F32),
            pltpu.VMEM((sz.rows, LANES), F32),
            pltpu.SemaphoreType.DMA((2 * wn,)),
            pltpu.SemaphoreType.DMA((2,)),
        ],
        compiler_params=pltpu.CompilerParams(vmem_limit_bytes=12 * MIB),
        cost_estimate=pl.CostEstimate(
            flops=40 * sz.rows * pad, bytes_accessed=20 * sz.rows * pad, transcendentals=0
        ),
        name="prepare",
    )(mode, *main, *extra)


def second_kernel(sz, chunk, skip, mode_ref, *refs):
    wn, n, pr = sz.wid, sz.hid, sz.part_rows
    refs = list(refs[skip:])

    def take(count):
        out, refs[:] = refs[:count], refs[count:]
        return out

    first = chunk == 0
    last = chunk == sz.chunks - 1
    p0, pc, d = take(wn), take(wn), take(wn)
    ready, stats, wg, wu, wd, a, b = take(7)
    acc_in = None if first else take(1)[0]
    gb_out = take(1)[0]
    if last:
        own_out = take(1)[0]
        sends = take(sz.send_arrays)
    else:
        acc_out, token = take(2)
    m_s, e_s, d_s, r_s, t_s, h_s, k_s, w_s, g_s, u_s, a_s, b_s, gb_s, acc_s, s_s = take(15)
    sem_i, sem_w, sem_u, sem_o = take(4)
    half, unit, pad = sz.half, sz.chunk_units, sz.unit_pad
    mode = mode_ref[0]
    size, size_h = block_of(unit), block_of(half)
    blocks, blocks_h = unit // size, half // size_h
    ring, ring_back = slots_of(DEPTH_DOWN, blocks_h), slots_of(DEPTH_BACK, blocks_h)
    carried = [] if first else [pltpu.make_async_copy(acc_in, acc_s, sem_i.at[2 * wn])]

    def write_out():
        if last:
            s_s[...] = acc_s[...].astype(BF16)
            outs = [pltpu.make_async_copy(acc_s.at[pl.ds(0, pr), :], own_out, sem_o.at[0])]
            if sz.slot_arrays == 1:
                outs.append(pltpu.make_async_copy(s_s, sends[0], sem_o.at[1]))
            else:
                for k in range(1, n):
                    outs.append(
                        pltpu.make_async_copy(
                            s_s.at[pl.ds(k * pr, pr), :], sends[k - 1], sem_o.at[k]
                        )
                    )
        else:
            outs = [
                pltpu.make_async_copy(acc_s, acc_out, sem_o.at[0]),
                pltpu.make_async_copy(acc_s.at[pl.ds(0, 8), pl.ds(0, LANES)], token, sem_o.at[1]),
            ]
        start_all(outs)
        wait_all(outs)

    @pl.when(mode == 1)
    def _():
        loads = part_copies(sz, pc, p0, m_s, e_s, sem_i)

        def copies(j):
            return (
                pltpu.make_async_copy(
                    wd.at[0, pl.ds(chunk * unit, unit), pl.ds(lane_start(j, size_h), size_h)],
                    w_s.at[lax.rem(j, ring)],
                    sem_w.at[lax.rem(j, ring)],
                ),
            )

        start_all(loads)
        start_all(carried)
        begin(copies, blocks_h, DEPTH_DOWN)
        wait_all(loads)
        inverse = inverse_of(sz, total(e_s, slice(None)))

        def act(i, _):
            gate = total(m_s, pl.ds(lane_start(i, size), size)) * inverse
            up = total(m_s, pl.ds(lane_start(i, size) + pad, size)) * inverse
            bend = jnp.tanh(ROOT * (gate + CUBIC * (gate * gate * gate)))
            h_s[:, pl.ds(lane_start(i, size), size)] = (
                0.5 * gate * (1.0 + bend) * up
            ).astype(BF16)
            return 0

        each(blocks, act)
        wait_all(carried)

        def step(j, _):
            arrive(copies, j, blocks_h, DEPTH_DOWN)
            where = pl.ds(lane_start(j, size_h), size_h)
            v = jnp.dot(h_s[...], w_s[lax.rem(j, ring)], preferred_element_type=F32)
            acc_s[:, where] = v if first else acc_s[:, where] + v
            return 0

        each(blocks_h, step)
        write_out()

    @pl.when(mode == 2)
    def _():
        loads = [pltpu.make_async_copy(ready, r_s, sem_i.at[2 * wn + 1])] + [
            pltpu.make_async_copy(d[j], d_s.at[j], sem_i.at[j]) for j in range(wn)
        ]
        more = [
            pltpu.make_async_copy(stats, t_s, sem_i.at[2 * wn + 2]),
            pltpu.make_async_copy(a, a_s, sem_i.at[2 * wn + 3]),
            pltpu.make_async_copy(b.at[chunk], b_s, sem_i.at[2 * wn + 4]),
        ]

        def copies(j):
            slot = lax.rem(j, ring_back)
            rows = pl.ds(j * size_h, size_h)
            cols = pl.ds(chunk * unit, unit)
            return (
                pltpu.make_async_copy(wg.at[0, rows, cols], g_s.at[slot], sem_w.at[slot]),
                pltpu.make_async_copy(wu.at[0, rows, cols], u_s.at[slot], sem_u.at[slot]),
            )

        start_all(loads)
        start_all(more)
        start_all(carried)
        begin(copies, blocks_h, DEPTH_BACK)
        wait_all(loads)

        def act(i, inner):
            where = pl.ds(lane_start(i, size), size)
            grad = total(d_s, where)
            h_s[:, where] = (grad * r_s[0, :, where]).astype(BF16)
            k_s[:, where] = (grad * r_s[1, :, where]).astype(BF16)
            return inner + jnp.sum(grad * r_s[2, :, where], 1, keepdims=True)

        inner = each(blocks, act, jnp.zeros((sz.rows, 1), F32))
        wait_all(more)
        wait_all(carried)
        low = t_s[...].astype(BF16)[:, : sz.rank]
        inverse = t_s[...][:, sz.rank:sz.rank + 1]
        grad_low = lax.dot_general(k_s[...], b_s[...], NT, preferred_element_type=F32)
        low_hi, low_mid, _ = split3(grad_low)
        low_hi, low_mid = low_hi.astype(BF16), low_mid.astype(BF16)

        def step(j, _):
            arrive(copies, j, blocks_h, DEPTH_BACK)
            where = pl.ds(lane_start(j, size_h), size_h)
            slot = lax.rem(j, ring_back)
            v = lax.dot_general(h_s[...], g_s[slot], NT, preferred_element_type=F32)
            v = v + lax.dot_general(k_s[...], u_s[slot], NT, preferred_element_type=F32)
            a_block = a_s[pl.ds(j * size_h, size_h), :][:, : sz.rank]
            v = v + lax.dot_general(low_hi, a_block, NT, preferred_element_type=F32)
            v = v + lax.dot_general(low_mid, a_block, NT, preferred_element_type=F32)
            acc_s[:, where] = v if first else acc_s[:, where] + v
            return 0

        each(blocks_h, step)
        gb_s[...] = lax.dot_general(low, k_s[...], TN, preferred_element_type=F32)
        out_b = pltpu.make_async_copy(gb_s, gb_out, sem_i.at[2 * wn + 5])
        out_b.start()
        if not first:
            inner = inner + acc_s[:, pl.ds(half, LANES)][:, :1]
            grad_low = grad_low + acc_s[:, pl.ds(half + LANES, LANES)][:, : sz.rank]
        if last:
            acc_s[:, pl.ds(half, LANES)] = at_lanes(
                (sz.rows, LANES), 0, split3(inner) + (inverse,)
            )
            hi, mid, _ = split3(grad_low * inverse)
            spread = jnp.zeros((pr, sz.low_lanes), F32)
            r_i = lax.broadcasted_iota(jnp.int32, (sz.rank, sz.low_lanes), 0)
            l_i = lax.broadcasted_iota(jnp.int32, (sz.rank, sz.low_lanes), 1)
            for j in range(n):
                for part, first_lane in ((hi, 2 * j * sz.rank), (mid, (2 * j + 1) * sz.rank)):
                    pick = jnp.where(l_i == r_i + first_lane, 1.0, 0.0).astype(BF16)
                    spread = spread + jnp.dot(
                        part[j * pr:(j + 1) * pr].astype(BF16), pick, preferred_element_type=F32
                    )
            for j in range(n):
                acc_s[pl.ds(j * pr, pr), pl.ds(half + LANES, sz.low_lanes)] = spread
        else:
            acc_s[:, pl.ds(half, LANES)] = at_lanes((sz.rows, LANES), 0, (inner,))
            r_i = lax.broadcasted_iota(jnp.int32, (sz.rank, LANES), 0)
            l_i = lax.broadcasted_iota(jnp.int32, (sz.rank, LANES), 1)
            pick = jnp.where(l_i == r_i, 1.0, 0.0).astype(BF16)
            wide = jnp.zeros((sz.rows, LANES), F32)
            for part in split3(grad_low):
                wide = wide + jnp.dot(part.astype(BF16), pick, preferred_element_type=F32)
            acc_s[:, pl.ds(half + LANES, LANES)] = wide
        write_out()
        out_b.wait()


def second_call(sz, chunk, mode, p0, pc, d, ready, stats, weights, acc, after=()):
    wg, wu, wd, a, b = weights
    wn, n, pr = sz.wid, sz.hid, sz.part_rows
    unit, half, pad = sz.chunk_units, sz.half, sz.unit_pad
    last = chunk == sz.chunks - 1
    size_h = block_of(half)
    blocks_h = half // size_h
    ring, ring_back = slots_of(DEPTH_DOWN, blocks_h), slots_of(DEPTH_BACK, blocks_h)
    wide = half + LANES + sz.low_lanes
    shapes = [jax.ShapeDtypeStruct((sz.rank, unit), F32)]
    if last:
        shapes.append(jax.ShapeDtypeStruct((pr, wide), F32))
        if sz.slot_arrays == n:
            shapes += [jax.ShapeDtypeStruct((pr, wide), BF16)] * (n - 1)
        else:
            shapes.append(jax.ShapeDtypeStruct((sz.rows, wide), BF16))
    else:
        shapes.append(jax.ShapeDtypeStruct((sz.rows, wide), F32))
        shapes.append(jax.ShapeDtypeStruct((8, LANES), F32))
    operands = [mode, *after, *p0, *pc, *d, ready, stats, wg, wu, wd, a, b]
    if chunk > 0:
        operands.append(acc)
    return pl.pallas_call(
        functools.partial(second_kernel, sz, chunk, len(after)),
        out_shape=shapes,
        in_specs=[SMEM] + [ANY] * (len(operands) - 1),
        out_specs=[ANY] * len(shapes),
        scratch_shapes=[
            pltpu.VMEM((wn, sz.rows, 2 * pad), BF16),
            pltpu.VMEM((wn, sz.rows, LANES), BF16),
            pltpu.VMEM((wn, sz.rows, pad), BF16),
            pltpu.VMEM((3, sz.rows, pad), F32),
            pltpu.VMEM((sz.rows, LANES), F32),
            pltpu.VMEM((sz.rows, unit), BF16),
            pltpu.VMEM((sz.rows, unit), BF16),
            pltpu.VMEM((ring, unit, size_h), BF16),
            pltpu.VMEM((ring_back, size_h, unit), BF16),
            pltpu.VMEM((ring_back, size_h, unit), BF16),
            pltpu.VMEM((half, LANES), BF16),
            pltpu.VMEM((sz.rank, unit), BF16),
            pltpu.VMEM((sz.rank, unit), F32),
            pltpu.VMEM((sz.rows, wide), F32),
            pltpu.VMEM((sz.rows, wide), BF16),
            pltpu.SemaphoreType.DMA((2 * wn + 6,)),
            pltpu.SemaphoreType.DMA((max(ring, ring_back),)),
            pltpu.SemaphoreType.DMA((ring_back,)),
            pltpu.SemaphoreType.DMA((max(n, 2),)),
        ],
        compiler_params=pltpu.CompilerParams(vmem_limit_bytes=44 * MIB),
        cost_estimate=pl.CostEstimate(
            flops=4 * sz.rows * half * unit, bytes_accessed=4 * half * unit, transcendentals=0
        ),
    )(*operands)


def finish_kernel(sz, skip, mode_ref, *refs):
    refs = refs[skip:]
    n, half = sz.hid, sz.half
    own = refs[0]
    got = refs[1:n]
    prev, saved, gain, out, payload, carry, low_out = refs[n:]
    mode = mode_ref[0]

    def before():
        if prev.shape[1] == half:
            return prev[...]
        return (
            prev[:, :half].astype(F32) + prev[:, pl.ds(half + LANES, half)].astype(F32)
        )

    def send(tail, v):
        hi = v.astype(BF16)
        payload[:, :half] = hi
        payload[:, pl.ds(half, LANES)] = tail
        carry[:, :half] = hi
        carry[:, pl.ds(half, LANES)] = tail
        carry[:, pl.ds(half + LANES, half)] = (v - hi.astype(F32)).astype(BF16)

    def summed():
        v = own[:, :half]
        for ref in got:
            v = v + ref[:, :half].astype(F32)
        return v

    @pl.when(mode == 1)
    def _():
        v = before() + summed()
        out[...] = v
        squares = jnp.sum(v * v, 1, keepdims=True)
        tail = at_lanes((sz.part_rows, LANES), sz.rank, split3(squares)).astype(BF16)
        send(tail, v)

    @pl.when(mode == 2)
    def _():
        marks = own[:, pl.ds(half, LANES)]
        inverse = sum_lanes(marks, 3, 1)
        low = own[:, pl.ds(half + LANES, sz.low_lanes)]
        for k, ref in enumerate(got):
            marks = marks + ref[:, pl.ds(half, LANES)].astype(F32)
            part = ref[:, pl.ds(half + LANES, sz.low_lanes)].astype(F32)
            low = low + pltpu.roll(part, sz.low_lanes - (k + 1) * 2 * sz.rank, 1)
        inner = sum_lanes(marks, 0, 3)
        factor = inverse * inverse * inner / sz.model
        v = before() + inverse * gain[...] * summed() - saved[...] * factor
        out[...] = v
        send(jnp.zeros((sz.part_rows, LANES), BF16), v)
        low_out[...] = low


def finish_call(sz, mode, own, got, prev, saved, gain, after=()):
    vm = pl.BlockSpec(memory_space=pltpu.VMEM)
    pr, half = sz.part_rows, sz.half
    return pl.pallas_call(
        functools.partial(finish_kernel, sz, len(after)),
        out_shape=[
            jax.ShapeDtypeStruct((pr, half), F32),
            jax.ShapeDtypeStruct((pr, half + LANES), BF16),
            jax.ShapeDtypeStruct((pr, 2 * half + LANES), BF16),
            jax.ShapeDtypeStruct((pr, sz.low_lanes), F32),
        ],
        in_specs=[SMEM] + [ANY] * len(after) + [vm] * (sz.hid + 3),
        out_specs=[vm] * 4,
        compiler_params=pltpu.CompilerParams(vmem_limit_bytes=10 * MIB),
        name="finish",
    )(mode, *after, own, *got, prev, saved, gain)


class Sizes:
    def __init__(self, mesh_sizes, part_rows, half, units, rank):
        self.seg, self.hid, self.wid = mesh_sizes
        self.part_rows, self.half, self.units, self.rank = part_rows, half, units, rank
        self.rows = part_rows * self.hid
        self.model = half * self.wid
        self.chunks = 2 if units % (2 * LANES) == 0 else 1
        self.chunk_units = units // self.chunks
        aligned = part_rows % 16 == 0
        self.unit_pad = -(-self.chunk_units // LANES) * LANES
        self.slot_arrays = self.hid if aligned else 1
        self.send_arrays = self.hid - 1 if aligned else 1
        self.low_lanes = 2 * rank * self.hid
        if self.low_lanes % LANES or self.seg < 4 or self.seg % 2:
            raise ValueError("unsupported mesh")

    def width(self, chunk):
        return 2 * self.unit_pad + (LANES if chunk == 0 else 0)

    def index(self, s, h, w):
        return (s * self.hid + h) * self.wid + w


def body(fwd_input, saved, cotan, norm_gain, w_gate, w_up, w_down, adapt_a, adapt_b):
    sizes = tuple(lax.axis_size(axis) for axis in AXES)
    section = lax.axis_index("segment")
    saved_rows = saved[0]
    part_rows, half = fwd_input.shape
    rank, units = adapt_b.shape[1:]
    sz = Sizes(sizes, part_rows, half, units, rank)
    seg, n, wn = sizes
    last = seg - 1
    weights = (
        w_gate, w_up, w_down, jnp.pad(adapt_a[0], ((0, 0), (0, LANES - rank))),
        jnp.stack(jnp.split(adapt_b[0], sz.chunks, 1)),
    )

    def route(block, moves, hid_shift=0, wid_shift=0):
        pairs = [
            (sz.index(s, h, w), sz.index(t, (h + hid_shift) % n, (w + wid_shift) % wn))
            for s, t in moves for h in range(n) for w in range(wn)
        ]
        return lax.ppermute(block, AXES, pairs)

    def stay(sections):
        return [(s, s) for s in sections]

    def rows_of(block, sections):
        return [block] + [route(block, stay(sections), k) for k in range(1, n)]

    def operands(slots):
        if sz.slot_arrays == n:
            return slots
        return [jnp.concatenate(slots)]

    def exchange(block, sections):
        return [block] + [route(block, stay(sections), 0, k) for k in range(1, wn)]

    def flag(*cases):
        mode = jnp.zeros((1,), jnp.int32)
        for value, sections in cases:
            for s in sections:
                mode = jnp.where(section == s, value, mode)
        return mode

    def pack(x, scale):
        squares = jnp.sum(x * x, 1, keepdims=True)
        hi = lax.reduce_precision(squares, 8, 7)
        mid = lax.reduce_precision(squares - hi, 8, 7)
        low = lax.reduce_precision(squares - hi - mid, 8, 7)
        tail = jnp.concatenate([hi, mid, low], 1)
        tail = jnp.pad(tail, ((0, 0), (rank, LANES - rank - 3)))
        return jnp.concatenate([x * scale, tail], 1).astype(BF16)

    def again_of(sections, parts):
        mode = flag((1, sections))
        made = [prepare_call(sz, mode, part, parts[0]) for part in parts]
        return [m[0] for m in made], made[0][1]

    def firsts(modes, slots, after=(), scale=None):
        made = []
        for c, mode in enumerate(modes):
            made.append(first_call(sz, c, mode, slots, weights, after, scale))
            after = made[-1][:1]
        return [m[0] for m in made], [m[1] for m in made]

    both = range(sz.chunks)
    gain = norm_gain
    begin_rows = jnp.where(section == 0, fwd_input, saved_rows)
    own_rows = rows_of(pack(begin_rows, gain), (0, last))
    slots = operands(own_rows)
    made, after = [], ()
    for c in both:
        made.append(first_call(sz, c, flag((1, (0, last))), slots, weights, after)[0])
        after = made[-1:]
    cot = jnp.pad(cotan, ((0, 0), (0, LANES))).astype(BF16)
    cot, _ = lax.optimization_barrier((cot, made[0]))
    cot_slots = operands(rows_of(cot, (last,)))
    grad_made = []
    for c in both:
        grad_made.append(first_call(sz, c, flag((2, (last,))), cot_slots, weights, after)[1])
        after = grad_made[-1:]
    fwd_parts = [exchange(m, (0, last)) for m in made]
    grad_parts = [exchange(m, (last,)) for m in grad_made]
    again, stats = again_of((last,), fwd_parts)
    packed = pack(saved_rows, gain)
    middle = tuple(range(1, last))
    mid_rows = rows_of(packed, middle)

    prev = jnp.where(section == 0, fwd_input, cotan)
    outs, lows, grad_bs = [], [], []
    after = ()
    for moment in range(seg):
        ahead, behind = moment, last - moment
        active = (ahead, behind)
        mode = flag((1, (ahead,)), (2, (behind,)))
        if moment > 0:
            made, grad_made = firsts([mode] * sz.chunks, slots, after, gain)
            fwd_parts, grad_parts = [], []
            for c in both:
                grad_parts.append(exchange(grad_made[c], (behind,)))
                fwd_parts.append(exchange(made[c], (ahead,)))
        acc, pieces_b, start, follow = None, [], None, ()
        for c in both:
            res = second_call(
                sz, c, mode, fwd_parts[0], fwd_parts[c], grad_parts[c], again[c], stats,
                weights, acc, follow,
            )
            pieces_b.append(res[0])
            if c < sz.chunks - 1:
                acc = res[1]
                if moment < 2:
                    moves = [(0, 1), (last, last - 1)] if moment == 0 else [(last - 1, last), (1, 0)]
                    start = route(res[2], moves)
                    follow = (start,)
        own, sends = res[1], res[2:]
        if sz.slot_arrays != n:
            sends = [sends[0][k * part_rows:(k + 1) * part_rows] for k in range(1, n)]
        got = [route(sends[k - 1], stay(active), -k) for k in range(1, n)]

        wait = ()
        if moment < 2:
            idle = middle if moment == 0 else (0,)
            source = mid_rows if moment == 0 else first_rows
            redo, _ = firsts(
                [flag((1, idle))] * sz.chunks, operands(source), follow + (own,)
            )
            parts = [exchange(m, idle) for m in redo]
            wait = tuple(redo)
        out, payload, carry, low = finish_call(
            sz, mode, own, got, prev, saved_rows, gain, wait
        )
        outs.append(out)
        lows.append(low)
        grad_bs.append(jnp.concatenate(pieces_b, 1))
        if moment < last:
            moves = [(ahead, ahead + 1), (behind, behind - 1)]
            prev = route(carry, moves)
            got = [prev] + [route(payload, moves, k) for k in range(1, n)]
            if sz.slot_arrays != n:
                got = [x[:, : half + LANES] for x in got]
            slots = operands(got)
            after = ()
        if moment == 0:
            again, stats = again_of(idle, parts)
            after += tuple(again)
            held, _ = lax.optimization_barrier((packed, out))
            first_rows = rows_of(held, (0, last))
        elif moment == 1:
            kept = again_of(idle, parts)
            after += tuple(kept[0])
        if moment == last - 1:
            again, stats = kept

    def choose(values, of):
        result = values[0]
        for moment in range(1, seg):
            result = jnp.where(section == of(moment), values[moment], result)
        return result

    fwd_out = choose(outs, lambda m: m)
    grad_in = choose(outs, lambda m: last - m)
    grad_b = choose(grad_bs, lambda m: last - m)
    low = choose(lows, lambda m: last - m)
    low = low.reshape(part_rows, n, 2, rank).sum(2)
    low = jnp.concatenate([low[:, k] for k in range(n)], 0)
    normed = jnp.concatenate(
        [
            jnp.where(
                section == last, x[:, :half], jnp.where(section == 0, z[:, :half], y[:, :half])
            )
            for x, y, z in zip(own_rows, mid_rows, first_rows)
        ],
        0,
    )
    grad_a = lax.dot_general(
        normed.astype(F32), low, TN, precision=lax.Precision.HIGHEST,
        preferred_element_type=F32,
    )
    return (fwd_out[None], grad_in[None], grad_a[None], grad_b[None])


def solution(mesh):
    placed = (
        P("hid", "wid"),
        P("segment", "hid", "wid"),
        P("hid", "wid"),
        P("segment", "wid"),
        P("segment", "wid", "hid"),
        P("segment", "wid", "hid"),
        P("segment", "hid", "wid"),
        P("segment", "wid", None),
        P("segment", None, "hid"),
    )
    return jax.shard_map(
        body,
        mesh=mesh,
        in_specs=placed,
        out_specs=(
            P("segment", "hid", "wid"),
            P("segment", "hid", "wid"),
            P("segment", "wid", None),
            P("segment", None, "hid"),
        ),
        check_vma=False,
    )
```

```python
import functools

import jax
import jax.numpy as jnp
from jax import lax
from jax.experimental import pallas as pl
from jax.experimental.pallas import tpu as pltpu
from jax.sharding import PartitionSpec as P


EPS = 1e-06
FIRST_COST = 16
DEPTH_FIRST = 2
MIB = 1 << 20
DEPTH_DOWN = 4
DEPTH_BACK = 2
LANES = 128
AXES = ("segment", "hid", "wid")
NT = (((1,), (1,)), ((), ()))
TN = (((0,), (0,)), ((), ()))
F32 = jnp.float32
BF16 = jnp.bfloat16
ROOT = 0.7978845608028654
CUBIC = 0.044715
ANY = pl.BlockSpec(memory_space=pl.ANY)
SMEM = pl.BlockSpec(memory_space=pltpu.SMEM)


def block_of(total, most=384):
    best = [d for d in range(LANES, most + 1, LANES) if total % d == 0]
    return best[-1] if best else total


def split3(v):
    hi = v.astype(BF16).astype(F32)
    mid = (v - hi).astype(BF16).astype(F32)
    return hi, mid, (v - hi - mid).astype(BF16).astype(F32)


def at_lanes(shape, first, parts):
    lane = lax.broadcasted_iota(jnp.int32, shape, 1)
    out = jnp.zeros(shape, F32)
    for i, part in enumerate(parts):
        out = jnp.where(lane == first + i, part, out)
    return out


def sum_lanes(v, first, count):
    lane = lax.broadcasted_iota(jnp.int32, v.shape, 1)
    return jnp.sum(jnp.where((lane >= first) & (lane < first + count), v, 0.0), 1, keepdims=True)


def lane_start(i, size):
    return pl.multiple_of(i * size, LANES) if size % LANES == 0 else i * size


def each(blocks, step, carry=0):
    if blocks == 1:
        return step(0, carry)
    return lax.fori_loop(0, blocks, step, carry)


def room(scratch, least, margin):
    total = margin
    for ref in scratch:
        if ref.dtype not in (BF16, F32):
            continue
        *lead, rows, lanes = ref.shape
        size = 2 if ref.dtype == BF16 else 4
        tile = 32 // size
        rows, lanes = -(-rows // tile) * tile, -(-lanes // LANES) * LANES
        for d in lead:
            rows *= d
        total += rows * lanes * size
    return max(total, least)


def when(enabled, condition):
    return pl.when(condition) if enabled else (lambda branch: None)


def slots_of(depth, blocks):
    return min(depth + 1, blocks)


def begin(copies, blocks, depth):
    for i in range(min(depth, blocks)):
        start_all(copies(i))


def arrive(copies, i, blocks, depth):
    wait_all(copies(i))
    if blocks > depth:

        @pl.when(i + depth < blocks)
        def _():
            start_all(copies(i + depth))


def start_all(copies):
    for copy in copies:
        copy.start()


def wait_all(copies):
    for copy in copies:
        copy.wait()


def first_kernel(sz, chunk, skip, scaled, kinds, mode_ref, *refs):
    refs = refs[skip:]
    n_slots = sz.slot_arrays
    slots = refs[:n_slots]
    wg, wu, wd, a, b = refs[n_slots:n_slots + 5]
    refs = refs[n_slots + 5:]
    gain = refs[0] if scaled else None
    out, grad_out, x_s, a_s, b_s, g_s, u_s, d_s, o_s, e_s, n_s, sem_x, sem_g, sem_u, sem_o = (
        refs[1:] if scaled else refs
    )
    half, unit, pad = sz.half, sz.chunk_units, sz.unit_pad
    rows = sz.rows // n_slots
    mode = mode_ref[0]
    size = block_of(unit)
    blocks = unit // size
    ring = slots_of(DEPTH_FIRST, blocks)
    loads = [
        pltpu.make_async_copy(
            slots[k].at[:, pl.ds(0, half + LANES)],
            x_s.at[pl.ds(k * rows, rows), :],
            sem_x.at[k],
        )
        for k in range(n_slots)
    ]

    def columns(ref, i):
        if blocks == 1:
            return ref.at[0]
        return ref.at[0, :, pl.ds(lane_start(i, size) + chunk * unit, size)]

    @when(1 in kinds, mode == 1)
    def _():
        more = [
            pltpu.make_async_copy(a, a_s, sem_x.at[n_slots]),
            pltpu.make_async_copy(b.at[chunk], b_s, sem_x.at[n_slots + 1]),
        ]

        def copies(i):
            slot = lax.rem(i, ring)
            return (
                pltpu.make_async_copy(columns(wg, i), g_s.at[slot], sem_g.at[slot]),
                pltpu.make_async_copy(columns(wu, i), u_s.at[slot], sem_u.at[slot]),
            )

        def store(i, part):
            where = pl.ds(lane_start(i, size) + part * pad, size if blocks > 1 else pad)
            return pltpu.make_async_copy(o_s.at[:, where], out.at[:, where], sem_o.at[part])

        if scaled:
            more.append(pltpu.make_async_copy(gain, n_s, sem_x.at[n_slots + 2]))
        start_all(loads + more)
        begin(copies, blocks, DEPTH_FIRST)
        wait_all(loads + more)
        if scaled:
            x_s[:, pl.ds(0, half)] = (x_s[:, :half].astype(F32) * n_s[...]).astype(BF16)
        low = jnp.dot(x_s[:, :half], a_s[...], preferred_element_type=F32).astype(BF16)
        e_s[...] = low + x_s[:, pl.ds(half, LANES)]
        if chunk == 0:
            tail = pltpu.make_async_copy(e_s, out.at[:, pl.ds(2 * pad, LANES)], sem_o.at[2])
            tail.start()

        def step(i, _):
            arrive(copies, i, blocks, DEPTH_FIRST)
            x = x_s[:, :half]
            slot = lax.rem(i, ring)
            gate = jnp.dot(x, g_s[slot], preferred_element_type=F32)
            up = jnp.dot(x, u_s[slot], preferred_element_type=F32)
            part = b_s[:, pl.ds(lane_start(i, size), size)]
            up = up + jnp.dot(e_s[...][:, : sz.rank], part, preferred_element_type=F32)
            o_s[:, pl.ds(lane_start(i, size), size)] = gate.astype(BF16)
            store(i, 0).start()
            o_s[:, pl.ds(lane_start(i, size) + pad, size)] = up.astype(BF16)
            store(i, 1).start()
            return 0

        each(blocks, step)
        for part in range(2):
            where = pl.ds(part * pad, pad)
            pltpu.make_async_copy(o_s.at[:, where], out.at[:, where], sem_o.at[part]).wait()
        if chunk == 0:
            tail.wait()

    @when(2 in kinds, mode == 2)
    def _():
        def copies(i):
            where = pl.ds(i * size + chunk * unit, size)
            slot = lax.rem(i, ring)
            return (pltpu.make_async_copy(wd.at[0, where, :], d_s.at[slot], sem_g.at[slot]),)

        def store(i):
            where = pl.ds(lane_start(i, size), size if blocks > 1 else pad)
            return pltpu.make_async_copy(o_s.at[:, where], grad_out.at[:, where], sem_o.at[0])

        start_all(loads)
        begin(copies, blocks, DEPTH_FIRST)
        wait_all(loads)

        def step(i, _):
            arrive(copies, i, blocks, DEPTH_FIRST)
            o_s[:, pl.ds(lane_start(i, size), size)] = lax.dot_general(
                x_s[:, :half], d_s[lax.rem(i, ring)], NT, preferred_element_type=F32
            ).astype(BF16)
            store(i).start()
            return 0

        each(blocks, step)
        where = pl.ds(0, pad)
        pltpu.make_async_copy(o_s.at[:, where], grad_out.at[:, where], sem_o.at[0]).wait()


def first_call(sz, chunk, mode, slots, weights, after=(), gain=None, kinds=(1, 2)):
    wg, wu, wd, a, b = weights
    unit, pad = sz.chunk_units, sz.unit_pad
    size = block_of(unit)
    blocks = unit // size
    ring = slots_of(DEPTH_FIRST, blocks)
    n = sz.slot_arrays
    extra = () if gain is None else (gain,)
    scratch = [
        pltpu.VMEM((sz.rows, sz.half + LANES), BF16),
        pltpu.VMEM((sz.half, LANES), BF16),
        pltpu.VMEM((sz.rank, unit), BF16),
        pltpu.VMEM((ring, sz.half, size), BF16),
        pltpu.VMEM((ring, sz.half, size), BF16),
        pltpu.VMEM((ring, size, sz.half), BF16),
        pltpu.VMEM((sz.rows, 2 * pad), BF16),
        pltpu.VMEM((sz.rows, LANES), BF16),
        pltpu.VMEM((1, sz.half), F32),
        pltpu.SemaphoreType.DMA((n + 3,)),
        pltpu.SemaphoreType.DMA((ring,)),
        pltpu.SemaphoreType.DMA((ring,)),
        pltpu.SemaphoreType.DMA((3,)),
    ]
    return pl.pallas_call(
        functools.partial(first_kernel, sz, chunk, len(after), gain is not None, kinds),
        out_shape=[
            jax.ShapeDtypeStruct((sz.rows, sz.width(chunk)), BF16),
            jax.ShapeDtypeStruct((sz.rows, pad), BF16),
        ],
        in_specs=[SMEM] + [ANY] * (len(after) + n + 5 + len(extra)),
        out_specs=[ANY] * 2,
        scratch_shapes=scratch,
        compiler_params=pltpu.CompilerParams(vmem_limit_bytes=room(scratch, 23 * MIB, sz.margin)),
        cost_estimate=pl.CostEstimate(
            flops=4 * sz.rows * sz.half * unit // FIRST_COST,
            bytes_accessed=4 * sz.half * unit // FIRST_COST,
            transcendentals=0,
        ),
    )(mode, *after, *slots, wg, wu, wd, a, b, *extra)


def total(ref, where):
    v = ref[0, :, where].astype(F32)
    for j in range(1, ref.shape[0]):
        v = v + ref[j, :, where].astype(F32)
    return v


def inverse_of(sz, extras):
    return lax.rsqrt(sum_lanes(extras, sz.rank, 3) / sz.model + EPS)


def part_copies(sz, main, extra, m_s, e_s, sem):
    out = []
    for j in range(sz.wid):
        out.append(
            pltpu.make_async_copy(
                extra[j].at[:, pl.ds(2 * sz.unit_pad, LANES)], e_s.at[j], sem.at[2 * j]
            )
        )
        out.append(
            pltpu.make_async_copy(
                main[j].at[:, pl.ds(0, 2 * sz.unit_pad)], m_s.at[j], sem.at[2 * j + 1]
            )
        )
    return out


def prepare_kernel(sz, mode_ref, *refs):
    wn = sz.wid
    main, extra = refs[:wn], refs[wn:2 * wn]
    out, stats, m_s, e_s, o_s, t_s, sem, sem_o = refs[2 * wn:]
    unit, pad = sz.chunk_units, sz.unit_pad
    size = block_of(unit)
    blocks = unit // size

    @pl.when(mode_ref[0] == 1)
    def _():
        loads = part_copies(sz, main, extra, m_s, e_s, sem)
        start_all(loads)
        wait_all(loads)
        extras = total(e_s, slice(None))
        inverse = inverse_of(sz, extras)
        lane = lax.broadcasted_iota(jnp.int32, (sz.rows, LANES), 1)
        t_s[...] = jnp.where(lane < sz.rank, extras * inverse, inverse)
        side = pltpu.make_async_copy(t_s, stats, sem_o.at[1])
        side.start()

        def step(i, _):
            where = pl.ds(lane_start(i, size), size)
            gate = total(m_s, where) * inverse
            up = total(m_s, pl.ds(lane_start(i, size) + pad, size)) * inverse
            bend = jnp.tanh(ROOT * (gate + CUBIC * (gate * gate * gate)))
            active = 0.5 * gate * (1.0 + bend)
            slope = 0.5 * (1.0 + bend) + 0.5 * gate * (1.0 - bend * bend) * (
                ROOT * (1.0 + 3.0 * CUBIC * (gate * gate))
            )
            o_s[0, :, where] = up * slope
            o_s[1, :, where] = active
            o_s[2, :, where] = up * (slope * gate + active)
            if blocks > 1:
                pltpu.make_async_copy(
                    o_s.at[:, :, where], out.at[:, :, where], sem_o.at[0]
                ).start()
            return 0

        each(blocks, step)
        done = pltpu.make_async_copy(o_s, out, sem_o.at[0])
        if blocks == 1:
            done.start()
        done.wait()
        side.wait()


def prepare_call(sz, mode, main, extra):
    wn, pad = sz.wid, sz.unit_pad
    return pl.pallas_call(
        functools.partial(prepare_kernel, sz),
        out_shape=[
            jax.ShapeDtypeStruct((3, sz.rows, pad), F32),
            jax.ShapeDtypeStruct((sz.rows, LANES), F32),
        ],
        in_specs=[SMEM] + [ANY] * (2 * wn),
        out_specs=[ANY] * 2,
        scratch_shapes=[
            pltpu.VMEM((wn, sz.rows, 2 * pad), BF16),
            pltpu.VMEM((wn, sz.rows, LANES), BF16),
            pltpu.VMEM((3, sz.rows, pad), F32),
            pltpu.VMEM((sz.rows, LANES), F32),
            pltpu.SemaphoreType.DMA((2 * wn,)),
            pltpu.SemaphoreType.DMA((2,)),
        ],
        compiler_params=pltpu.CompilerParams(vmem_limit_bytes=12 * MIB),
        cost_estimate=pl.CostEstimate(
            flops=40 * sz.rows * pad, bytes_accessed=20 * sz.rows * pad, transcendentals=0
        ),
        name="prepare",
    )(mode, *main, *extra)


def second_kernel(sz, chunk, skip, mode_ref, *refs):
    wn, n, pr = sz.wid, sz.hid, sz.part_rows
    refs = list(refs[skip:])

    def take(count):
        out, refs[:] = refs[:count], refs[count:]
        return out

    first = chunk == 0
    last = chunk == sz.chunks - 1
    p0, pc, d = take(wn), take(wn), take(wn)
    ready, stats, wg, wu, wd, a, b = take(7)
    acc_in = None if first else take(1)[0]
    gb_out = take(1)[0]
    if last:
        own_out = take(1)[0]
        sends = take(sz.send_arrays)
    else:
        acc_out, token = take(2)
    m_s, e_s, d_s, r_s, t_s, h_s, k_s, w_s, g_s, u_s, a_s, b_s, gb_s, acc_s, s_s = take(15)
    sem_i, sem_w, sem_u, sem_o = take(4)
    half, unit, pad = sz.half, sz.chunk_units, sz.unit_pad
    mode = mode_ref[0]
    size, size_h = block_of(unit), block_of(half)
    blocks, blocks_h = unit // size, half // size_h
    ring, ring_back = slots_of(DEPTH_DOWN, blocks_h), slots_of(DEPTH_BACK, blocks_h)
    carried = [] if first else [pltpu.make_async_copy(acc_in, acc_s, sem_i.at[2 * wn])]

    def parts_of(where):
        if not last:
            return [pltpu.make_async_copy(acc_s.at[:, where], acc_out.at[:, where], sem_o.at[0])]
        outs = [
            pltpu.make_async_copy(
                acc_s.at[pl.ds(0, pr), where], own_out.at[:, where], sem_o.at[0]
            )
        ]
        if sz.slot_arrays == 1:
            outs.append(
                pltpu.make_async_copy(s_s.at[:, where], sends[0].at[:, where], sem_o.at[1])
            )
        else:
            for k in range(1, n):
                outs.append(
                    pltpu.make_async_copy(
                        s_s.at[pl.ds(k * pr, pr), where], sends[k - 1].at[:, where], sem_o.at[k]
                    )
                )
        return outs

    def emit(where):
        if last:
            s_s[:, where] = acc_s[:, where].astype(BF16)
        start_all(parts_of(where))

    def write_out():
        emit(pl.ds(half, acc_s.shape[1] - half))
        if not last:
            mark = pltpu.make_async_copy(
                acc_s.at[pl.ds(0, 8), pl.ds(0, LANES)], token, sem_o.at[1]
            )
            mark.start()
            mark.wait()
        wait_all(parts_of(pl.ds(0, acc_s.shape[1])))

    @pl.when(mode == 1)
    def _():
        loads = part_copies(sz, pc, p0, m_s, e_s, sem_i)

        def copies(j):
            return (
                pltpu.make_async_copy(
                    wd.at[0, pl.ds(chunk * unit, unit), pl.ds(lane_start(j, size_h), size_h)],
                    w_s.at[lax.rem(j, ring)],
                    sem_w.at[lax.rem(j, ring)],
                ),
            )

        start_all(loads)
        start_all(carried)
        begin(copies, blocks_h, DEPTH_DOWN)
        wait_all(loads)
        inverse = inverse_of(sz, total(e_s, slice(None)))

        def act(i, _):
            gate = total(m_s, pl.ds(lane_start(i, size), size)) * inverse
            up = total(m_s, pl.ds(lane_start(i, size) + pad, size)) * inverse
            bend = jnp.tanh(ROOT * (gate + CUBIC * (gate * gate * gate)))
            h_s[:, pl.ds(lane_start(i, size), size)] = (
                0.5 * gate * (1.0 + bend) * up
            ).astype(BF16)
            return 0

        each(blocks, act)
        wait_all(carried)

        def step(j, _):
            arrive(copies, j, blocks_h, DEPTH_DOWN)
            where = pl.ds(lane_start(j, size_h), size_h)
            v = jnp.dot(h_s[...], w_s[lax.rem(j, ring)], preferred_element_type=F32)
            acc_s[:, where] = v if first else acc_s[:, where] + v
            emit(where)
            return 0

        each(blocks_h, step)
        write_out()

    @pl.when(mode == 2)
    def _():
        loads = [pltpu.make_async_copy(ready, r_s, sem_i.at[2 * wn + 1])] + [
            pltpu.make_async_copy(d[j], d_s.at[j], sem_i.at[j]) for j in range(wn)
        ]
        more = [
            pltpu.make_async_copy(stats, t_s, sem_i.at[2 * wn + 2]),
            pltpu.make_async_copy(a, a_s, sem_i.at[2 * wn + 3]),
            pltpu.make_async_copy(b.at[chunk], b_s, sem_i.at[2 * wn + 4]),
        ]

        def copies(j):
            slot = lax.rem(j, ring_back)
            rows = pl.ds(j * size_h, size_h)
            cols = pl.ds(chunk * unit, unit)
            return (
                pltpu.make_async_copy(wg.at[0, rows, cols], g_s.at[slot], sem_w.at[slot]),
                pltpu.make_async_copy(wu.at[0, rows, cols], u_s.at[slot], sem_u.at[slot]),
            )

        start_all(loads)
        start_all(more)
        start_all(carried)
        begin(copies, blocks_h, DEPTH_BACK)
        wait_all(loads)

        def act(i, inner):
            where = pl.ds(lane_start(i, size), size)
            grad = total(d_s, where)
            h_s[:, where] = (grad * r_s[0, :, where]).astype(BF16)
            k_s[:, where] = (grad * r_s[1, :, where]).astype(BF16)
            return inner + jnp.sum(grad * r_s[2, :, where], 1, keepdims=True)

        inner = each(blocks, act, jnp.zeros((sz.rows, 1), F32))
        wait_all(more)
        wait_all(carried)
        low = t_s[...].astype(BF16)[:, : sz.rank]
        inverse = t_s[...][:, sz.rank:sz.rank + 1]
        grad_low = lax.dot_general(k_s[...], b_s[...], NT, preferred_element_type=F32)
        low_hi, low_mid, _ = split3(grad_low)
        low_hi, low_mid = low_hi.astype(BF16), low_mid.astype(BF16)

        def step(j, _):
            arrive(copies, j, blocks_h, DEPTH_BACK)
            where = pl.ds(lane_start(j, size_h), size_h)
            slot = lax.rem(j, ring_back)
            v = lax.dot_general(h_s[...], g_s[slot], NT, preferred_element_type=F32)
            v = v + lax.dot_general(k_s[...], u_s[slot], NT, preferred_element_type=F32)
            a_block = a_s[pl.ds(j * size_h, size_h), :][:, : sz.rank]
            v = v + lax.dot_general(low_hi, a_block, NT, preferred_element_type=F32)
            v = v + lax.dot_general(low_mid, a_block, NT, preferred_element_type=F32)
            acc_s[:, where] = v if first else acc_s[:, where] + v
            emit(where)
            return 0

        each(blocks_h, step)
        gb_s[...] = lax.dot_general(low, k_s[...], TN, preferred_element_type=F32)
        out_b = pltpu.make_async_copy(gb_s, gb_out, sem_i.at[2 * wn + 5])
        out_b.start()
        if not first:
            inner = inner + acc_s[:, pl.ds(half, LANES)][:, :1]
            grad_low = grad_low + acc_s[:, pl.ds(half + LANES, LANES)][:, : sz.rank]
        if last:
            acc_s[:, pl.ds(half, LANES)] = at_lanes(
                (sz.rows, LANES), 0, split3(inner) + (inverse,)
            )
            hi, mid, _ = split3(grad_low * inverse)
            spread = jnp.zeros((pr, sz.low_lanes), F32)
            r_i = lax.broadcasted_iota(jnp.int32, (sz.rank, sz.low_lanes), 0)
            l_i = lax.broadcasted_iota(jnp.int32, (sz.rank, sz.low_lanes), 1)
            for j in range(n):
                for part, first_lane in ((hi, 2 * j * sz.rank), (mid, (2 * j + 1) * sz.rank)):
                    pick = jnp.where(l_i == r_i + first_lane, 1.0, 0.0).astype(BF16)
                    spread = spread + jnp.dot(
                        part[j * pr:(j + 1) * pr].astype(BF16), pick, preferred_element_type=F32
                    )
            for j in range(n):
                acc_s[pl.ds(j * pr, pr), pl.ds(half + LANES, sz.low_lanes)] = spread
        else:
            acc_s[:, pl.ds(half, LANES)] = at_lanes((sz.rows, LANES), 0, (inner,))
            r_i = lax.broadcasted_iota(jnp.int32, (sz.rank, LANES), 0)
            l_i = lax.broadcasted_iota(jnp.int32, (sz.rank, LANES), 1)
            pick = jnp.where(l_i == r_i, 1.0, 0.0).astype(BF16)
            wide = jnp.zeros((sz.rows, LANES), F32)
            for part in split3(grad_low):
                wide = wide + jnp.dot(part.astype(BF16), pick, preferred_element_type=F32)
            acc_s[:, pl.ds(half + LANES, LANES)] = wide
        write_out()
        out_b.wait()


def second_call(sz, chunk, mode, p0, pc, d, ready, stats, weights, acc, after=()):
    wg, wu, wd, a, b = weights
    wn, n, pr = sz.wid, sz.hid, sz.part_rows
    unit, half, pad = sz.chunk_units, sz.half, sz.unit_pad
    last = chunk == sz.chunks - 1
    size_h = block_of(half)
    blocks_h = half // size_h
    ring, ring_back = slots_of(DEPTH_DOWN, blocks_h), slots_of(DEPTH_BACK, blocks_h)
    wide = half + LANES + sz.low_lanes
    shapes = [jax.ShapeDtypeStruct((sz.rank, unit), F32)]
    if last:
        shapes.append(jax.ShapeDtypeStruct((pr, wide), F32))
        if sz.slot_arrays == n:
            shapes += [jax.ShapeDtypeStruct((pr, wide), BF16)] * (n - 1)
        else:
            shapes.append(jax.ShapeDtypeStruct((sz.rows, wide), BF16))
    else:
        shapes.append(jax.ShapeDtypeStruct((sz.rows, wide), F32))
        shapes.append(jax.ShapeDtypeStruct((8, LANES), F32))
    operands = [mode, *after, *p0, *pc, *d, ready, stats, wg, wu, wd, a, b]
    if chunk > 0:
        operands.append(acc)
    scratch = [
        pltpu.VMEM((wn, sz.rows, 2 * pad), BF16),
        pltpu.VMEM((wn, sz.rows, LANES), BF16),
        pltpu.VMEM((wn, sz.rows, pad), BF16),
        pltpu.VMEM((3, sz.rows, pad), F32),
        pltpu.VMEM((sz.rows, LANES), F32),
        pltpu.VMEM((sz.rows, unit), BF16),
        pltpu.VMEM((sz.rows, unit), BF16),
        pltpu.VMEM((ring, unit, size_h), BF16),
        pltpu.VMEM((ring_back, size_h, unit), BF16),
        pltpu.VMEM((ring_back, size_h, unit), BF16),
        pltpu.VMEM((half, LANES), BF16),
        pltpu.VMEM((sz.rank, unit), BF16),
        pltpu.VMEM((sz.rank, unit), F32),
        pltpu.VMEM((sz.rows, wide), F32),
        pltpu.VMEM((sz.rows, wide), BF16),
        pltpu.SemaphoreType.DMA((2 * wn + 6,)),
        pltpu.SemaphoreType.DMA((max(ring, ring_back),)),
        pltpu.SemaphoreType.DMA((ring_back,)),
        pltpu.SemaphoreType.DMA((max(n, 2),)),
    ]
    return pl.pallas_call(
        functools.partial(second_kernel, sz, chunk, len(after)),
        out_shape=shapes,
        in_specs=[SMEM] + [ANY] * (len(operands) - 1),
        out_specs=[ANY] * len(shapes),
        scratch_shapes=scratch,
        compiler_params=pltpu.CompilerParams(vmem_limit_bytes=room(scratch, 37 * MIB, sz.margin)),
        cost_estimate=pl.CostEstimate(
            flops=4 * sz.rows * half * unit, bytes_accessed=4 * half * unit, transcendentals=0
        ),
    )(*operands)


def finish_kernel(sz, skip, mode_ref, *refs):
    refs = refs[skip:]
    n, half = sz.hid, sz.half
    own = refs[0]
    got = refs[1:n]
    prev, saved, gain, out, payload, carry, low_out = refs[n:]
    mode = mode_ref[0]

    def before():
        if prev.shape[1] == half:
            return prev[...]
        return (
            prev[:, :half].astype(F32) + prev[:, pl.ds(half + LANES, half)].astype(F32)
        )

    def send(tail, v):
        hi = v.astype(BF16)
        payload[:, :half] = hi
        payload[:, pl.ds(half, LANES)] = tail
        carry[:, :half] = hi
        carry[:, pl.ds(half, LANES)] = tail
        carry[:, pl.ds(half + LANES, half)] = (v - hi.astype(F32)).astype(BF16)

    def summed():
        v = own[:, :half]
        for ref in got:
            v = v + ref[:, :half].astype(F32)
        return v

    @pl.when(mode == 1)
    def _():
        v = before() + summed()
        out[...] = v
        squares = jnp.sum(v * v, 1, keepdims=True)
        tail = at_lanes((sz.part_rows, LANES), sz.rank, split3(squares)).astype(BF16)
        send(tail, v)

    @pl.when(mode == 2)
    def _():
        marks = own[:, pl.ds(half, LANES)]
        inverse = sum_lanes(marks, 3, 1)
        low = own[:, pl.ds(half + LANES, sz.low_lanes)]
        for k, ref in enumerate(got):
            marks = marks + ref[:, pl.ds(half, LANES)].astype(F32)
            part = ref[:, pl.ds(half + LANES, sz.low_lanes)].astype(F32)
            low = low + pltpu.roll(part, sz.low_lanes - (k + 1) * 2 * sz.rank, 1)
        inner = sum_lanes(marks, 0, 3)
        factor = inverse * inverse * inner / sz.model
        v = before() + inverse * gain[...] * summed() - saved[...] * factor
        out[...] = v
        send(jnp.zeros((sz.part_rows, LANES), BF16), v)
        low_out[...] = low


def finish_call(sz, mode, own, got, prev, saved, gain, after=()):
    vm = pl.BlockSpec(memory_space=pltpu.VMEM)
    pr, half = sz.part_rows, sz.half
    return pl.pallas_call(
        functools.partial(finish_kernel, sz, len(after)),
        out_shape=[
            jax.ShapeDtypeStruct((pr, half), F32),
            jax.ShapeDtypeStruct((pr, half + LANES), BF16),
            jax.ShapeDtypeStruct((pr, 2 * half + LANES), BF16),
            jax.ShapeDtypeStruct((pr, sz.low_lanes), F32),
        ],
        in_specs=[SMEM] + [ANY] * len(after) + [vm] * (sz.hid + 3),
        out_specs=[vm] * 4,
        compiler_params=pltpu.CompilerParams(vmem_limit_bytes=10 * MIB),
        name="finish",
    )(mode, *after, own, *got, prev, saved, gain)


class Sizes:
    def __init__(self, mesh_sizes, part_rows, half, units, rank):
        self.seg, self.hid, self.wid = mesh_sizes
        self.part_rows, self.half, self.units, self.rank = part_rows, half, units, rank
        self.rows = part_rows * self.hid
        self.model = half * self.wid
        self.chunks = 2 if units % (2 * LANES) == 0 else 1
        self.chunk_units = units // self.chunks
        aligned = part_rows % 16 == 0
        self.unit_pad = -(-self.chunk_units // LANES) * LANES
        self.margin = (2 if self.unit_pad == self.chunk_units else 10) * MIB
        self.slot_arrays = self.hid if aligned else 1
        self.send_arrays = self.hid - 1 if aligned else 1
        self.low_lanes = 2 * rank * self.hid
        if self.low_lanes % LANES or self.seg < 4 or self.seg % 2:
            raise ValueError("unsupported mesh")

    def width(self, chunk):
        return 2 * self.unit_pad + (LANES if chunk == 0 else 0)

    def index(self, s, h, w):
        return (s * self.hid + h) * self.wid + w


def body(fwd_input, saved, cotan, norm_gain, w_gate, w_up, w_down, adapt_a, adapt_b):
    sizes = tuple(lax.axis_size(axis) for axis in AXES)
    section = lax.axis_index("segment")
    saved_rows = saved[0]
    part_rows, half = fwd_input.shape
    rank, units = adapt_b.shape[1:]
    sz = Sizes(sizes, part_rows, half, units, rank)
    seg, n, wn = sizes
    last = seg - 1
    weights = (
        w_gate, w_up, w_down, jnp.pad(adapt_a[0], ((0, 0), (0, LANES - rank))),
        jnp.stack(jnp.split(adapt_b[0], sz.chunks, 1)),
    )

    def route(block, moves, hid_shift=0, wid_shift=0):
        pairs = [
            (sz.index(s, h, w), sz.index(t, (h + hid_shift) % n, (w + wid_shift) % wn))
            for s, t in moves for h in range(n) for w in range(wn)
        ]
        return lax.ppermute(block, AXES, pairs)

    def stay(sections):
        return [(s, s) for s in sections]

    def rows_of(block, sections):
        return [block] + [route(block, stay(sections), k) for k in range(1, n)]

    def operands(slots):
        if sz.slot_arrays == n:
            return slots
        return [jnp.concatenate(slots)]

    def exchange(block, sections):
        return [block] + [route(block, stay(sections), 0, k) for k in range(1, wn)]

    def flag(*cases):
        mode = jnp.zeros((1,), jnp.int32)
        for value, sections in cases:
            for s in sections:
                mode = jnp.where(section == s, value, mode)
        return mode

    def pack(x, scale):
        squares = jnp.sum(x * x, 1, keepdims=True)
        hi = lax.reduce_precision(squares, 8, 7)
        mid = lax.reduce_precision(squares - hi, 8, 7)
        low = lax.reduce_precision(squares - hi - mid, 8, 7)
        tail = jnp.concatenate([hi, mid, low], 1)
        tail = jnp.pad(tail, ((0, 0), (rank, LANES - rank - 3)))
        return jnp.concatenate([x * scale, tail], 1).astype(BF16)

    def again_of(sections, parts):
        mode = flag((1, sections))
        made = [prepare_call(sz, mode, part, parts[0]) for part in parts]
        return [m[0] for m in made], made[0][1]

    def firsts(modes, slots, after=(), scale=None):
        made = []
        for c, mode in enumerate(modes):
            kinds = (1,) if scale is None else (1, 2)
            made.append(first_call(sz, c, mode, slots, weights, after, scale, kinds))
            after = made[-1][:1]
        return [m[0] for m in made], [m[1] for m in made]

    both = range(sz.chunks)
    gain = norm_gain
    begin_rows = jnp.where(section == 0, fwd_input, saved_rows)
    own_rows = rows_of(pack(begin_rows, gain), (0, last))
    slots = operands(own_rows)
    made, after = [], ()
    for c in both:
        made.append(first_call(sz, c, flag((1, (0, last))), slots, weights, after, kinds=(1,))[0])
        after = made[-1:]
    cot = jnp.pad(cotan, ((0, 0), (0, LANES))).astype(BF16)
    cot, _ = lax.optimization_barrier((cot, made[0]))
    cot_slots = operands(rows_of(cot, (last,)))
    grad_made = []
    for c in both:
        grad_made.append(
            first_call(sz, c, flag((2, (last,))), cot_slots, weights, after, kinds=(2,))[1]
        )
        after = grad_made[-1:]
    fwd_parts = [exchange(m, (0, last)) for m in made]
    grad_parts = [exchange(m, (last,)) for m in grad_made]
    again, stats = again_of((last,), fwd_parts)
    packed = pack(saved_rows, gain)
    middle = tuple(range(1, last))
    mid_rows = rows_of(packed, middle)

    prev = jnp.where(section == 0, fwd_input, cotan)
    outs, lows, grad_bs = [], [], []
    after = ()
    for moment in range(seg):
        ahead, behind = moment, last - moment
        active = (ahead, behind)
        mode = flag((1, (ahead,)), (2, (behind,)))
        if moment > 0:
            made, grad_made = firsts([mode] * sz.chunks, slots, after, gain)
            fwd_parts, grad_parts = [], []
            for c in both:
                grad_parts.append(exchange(grad_made[c], (behind,)))
                fwd_parts.append(exchange(made[c], (ahead,)))
        acc, pieces_b, start, follow = None, [], None, ()
        for c in both:
            res = second_call(
                sz, c, mode, fwd_parts[0], fwd_parts[c], grad_parts[c], again[c], stats,
                weights, acc, follow,
            )
            pieces_b.append(res[0])
            if c < sz.chunks - 1:
                acc = res[1]
                if moment < 2:
                    moves = [(0, 1), (last, last - 1)] if moment == 0 else [(last - 1, last), (1, 0)]
                    start = route(res[2], moves)
                    follow = (start,)
        own, sends = res[1], res[2:]
        if sz.slot_arrays != n:
            sends = [sends[0][k * part_rows:(k + 1) * part_rows] for k in range(1, n)]
        got = [route(sends[k - 1], stay(active), -k) for k in range(1, n)]

        wait = ()
        if moment < 2:
            idle = middle if moment == 0 else (0,)
            source = mid_rows if moment == 0 else first_rows
            redo, _ = firsts(
                [flag((1, idle))] * sz.chunks, operands(source), follow + (own,)
            )
            parts = [exchange(m, idle) for m in redo]
            wait = tuple(redo)
        out, payload, carry, low = finish_call(
            sz, mode, own, got, prev, saved_rows, gain, wait
        )
        outs.append(out)
        lows.append(low)
        grad_bs.append(jnp.concatenate(pieces_b, 1))
        if moment < last:
            moves = [(ahead, ahead + 1), (behind, behind - 1)]
            prev = route(carry, moves)
            got = [prev] + [route(payload, moves, k) for k in range(1, n)]
            if sz.slot_arrays != n:
                got = [x[:, : half + LANES] for x in got]
            slots = operands(got)
            after = ()
        if moment == 0:
            again, stats = again_of(idle, parts)
            after += tuple(again)
            held, _ = lax.optimization_barrier((packed, out))
            first_rows = rows_of(held, (0, last))
        elif moment == 1:
            kept = again_of(idle, parts)
            after += tuple(kept[0])
        if moment == last - 1:
            again, stats = kept

    def choose(values, of):
        result = values[0]
        for moment in range(1, seg):
            result = jnp.where(section == of(moment), values[moment], result)
        return result

    fwd_out = choose(outs, lambda m: m)
    grad_in = choose(outs, lambda m: last - m)
    grad_b = choose(grad_bs, lambda m: last - m)
    low = choose(lows, lambda m: last - m)
    low = low.reshape(part_rows, n, 2, rank).sum(2)
    low = jnp.concatenate([low[:, k] for k in range(n)], 0)
    normed = jnp.concatenate(
        [
            jnp.where(
                section == last, x[:, :half], jnp.where(section == 0, z[:, :half], y[:, :half])
            )
            for x, y, z in zip(own_rows, mid_rows, first_rows)
        ],
        0,
    )
    grad_a = lax.dot_general(
        normed.astype(F32), low, TN, precision=lax.Precision.HIGHEST,
        preferred_element_type=F32,
    )
    return (fwd_out[None], grad_in[None], grad_a[None], grad_b[None])


def solution(mesh):
    placed = (
        P("hid", "wid"),
        P("segment", "hid", "wid"),
        P("hid", "wid"),
        P("segment", "wid"),
        P("segment", "wid", "hid"),
        P("segment", "wid", "hid"),
        P("segment", "hid", "wid"),
        P("segment", "wid", None),
        P("segment", None, "hid"),
    )
    return jax.shard_map(
        body,
        mesh=mesh,
        in_specs=placed,
        out_specs=(
            P("segment", "hid", "wid"),
            P("segment", "hid", "wid"),
            P("segment", "wid", None),
            P("segment", None, "hid"),
        ),
        check_vma=False,
    )
```
